128 devices in a mesh: dp: 32 (over x, z, core), label: 4 (over y).
Axes of the slice: x: 4, y: 4, z: 4, core: 2. Of those that a mesh axis runs over, the one named last changes fastest.
Arguments:
- queries: bfloat16 [131072, 256], P('dp'), may hold values from -6 to 6
- cluster: int32 [131072, 1], P('dp'), may hold values from 0 to 63; in each aligned block of 4096 rows (0 to 4095, 4096 to 8191, ...) at most 128 rows name the same one
- anchor_latent: bfloat16 [131072, 256], P('dp'), may hold values from -6 to 6
- anchor_labels: bfloat16 [131072, 1024], P('dp', 'label'), may hold values from -6 to 6
- tile_list: int32 [64, 16], P('dp'), may hold values from 0 to 1023, as said below
Outputs:
- predicted: bfloat16 [131072, 1024], P('dp', 'label')
The draws below stay inside these ranges and needn't reach their ends.
Inputs may be any that keep to these rules, and one draw needn't show every extreme that they name: `tile_list`: the 32 tiles listed in the rows of the blocks that one index of dp owns (rows d * 2 to d * 2 + 1 for index d) include at most 2 tiles held by any one index of dp (tile t is held by index t // 32), and exactly 2 from some index, for every d. `cluster`: among the rows of one index of dp no block is named more than 128 times; some block is named exactly 128 times. Block b is owned by index b // 2.
All inputs are finite; a program needn't handle non-finite values.
Results may differ from the reference program's by a relative error of at most 0.0097.
Values may be sent and summed in bfloat16 or wider, within the bound.
No kernel may reach another device: no remote copies, remote signals or barrier semaphores. Data moves between devices by JAX's collectives and lax.ppermute only.
A program may use at most 128 MiB of HBM per device.

```python
import math
import jax
import jax.numpy as jnp
import numpy as np
from jax import lax

LAT = 256
LABELS = 1024
TILE = 128
BLK_DEV = 2
TPB = 16
Q_DEV = 4096
NB = 64
CAPB = 128
ROWS_BLK = 4096
TILES_DEV = 32
NTILES = 1024
FETCH = 2
QUERIES = 131072
ANCHORS = 131072
N_DP = 32


def draw_tile_list(key, part):
    request_count = BLK_DEV * TPB
    key_list = jax.random.split(key, 5)
    hot_pick = jnp.min(jax.random.randint(key_list[0], (3, N_DP), 0, N_DP), axis=0)
    ordering = jax.random.permutation(key_list[1], N_DP)
    hot_owner = ordering[hot_pick]
    others = jax.vmap(lambda subkey: jax.random.permutation(subkey, N_DP - 1))(jax.random.split(key_list[2], N_DP))
    slot_ids = jnp.arange(request_count)
    positions = jnp.maximum(slot_ids - FETCH, 0) % (N_DP - 1)
    other_owner = (hot_owner[:, None] + 1 + jnp.take_along_axis(others, jnp.broadcast_to(positions[None, :], (N_DP, request_count)), axis=1)) % N_DP
    owner_ids = jnp.where(slot_ids[None, :] < FETCH, hot_owner[:, None], other_owner)
    shuffles = jax.vmap(lambda subkey: jax.random.permutation(subkey, request_count))(jax.random.split(key_list[3], N_DP))
    owner_ids = jnp.take_along_axis(owner_ids, shuffles, axis=1)
    local_ids = jax.random.randint(key_list[4], (N_DP, request_count), 0, TILES_DEV)
    return (owner_ids * TILES_DEV + local_ids).astype(jnp.int32).reshape(NB, TPB)


def shard_levels(stream_key, shape, cuts, smallest, high):
    def one(dim, parts):
        heights = jax.random.uniform(jax.random.fold_in(jax.random.fold_in(stream_key, 6), dim), (parts,), jnp.float32, smallest / len(cuts), high / len(cuts))
        return jnp.repeat(jnp.exp(heights), shape[dim] // parts).reshape((-1,) + (1,) * (len(shape) - dim - 1))

    gain = one(*cuts[0])
    for cut in cuts[1:]:
        gain = gain * one(*cut)
    return gain


def routed_block(stream_key, own, number, rows, number_of, top, most, slope):
    order = jax.random.permutation(stream_key, number_of)
    crowded, common = load_shares(number_of, rows * top, most, slope, True), load_shares(number_of, rows * top, most, slope, False)
    places = jnp.arange(number_of)

    def named(lengths, turn):
        used = int((lengths > 0).sum())
        fixed = max(1, used // 4)
        passed = fixed + (places - fixed + turn * (used - fixed)) % max(1, number_of - fixed)
        return jnp.zeros((number_of,), jnp.int32).at[order[jnp.where(places < fixed, places, passed)]].set(jnp.asarray(lengths, jnp.int32))

    lengths = jnp.where(number % 4 == 0, named(crowded, number // 4), named(common, number - number // 4 - 1))
    mixed = jax.random.permutation(jax.random.fold_in(own, 3), number_of)
    giver, taker = mixed[0:number_of // 2 * 2:2], mixed[1:number_of // 2 * 2:2]
    room = jnp.minimum(lengths[giver] - 1, most - lengths[taker]) // 2
    room = jnp.where((giver == order[0]) | (taker == order[0]) | (lengths[taker] == 0), 0, jnp.maximum(room, 0))
    passed = jax.random.randint(jax.random.fold_in(own, 4), (number_of // 2,), 0, 1 << 20) % (room + 1)
    lengths = lengths.at[giver].add(-passed).at[taker].add(passed)
    labels = jnp.searchsorted(jnp.cumsum(lengths), jnp.arange(rows * top), side="right").astype(jnp.int32)
    listing = labels.reshape(top, rows).T
    listing = listing[jax.random.permutation(jax.random.fold_in(own, 1), rows)]
    turn = jax.random.randint(jax.random.fold_in(own, 2), (rows, 1), 0, top)
    return jnp.take_along_axis(listing, (jnp.arange(top)[None, :] + turn) % top, axis=1)


def load_shares(amount, total, bound, skew, full):
    loads = [(1 << 20) // math.isqrt(standing ** skew) + 1 for standing in range(1, amount + 1)]
    largest = bound if full else min(bound, max(-(-total // amount), total * loads[0] // sum(loads)))
    least = 1 if total - largest >= amount - 1 else 0
    given, rest = [largest] + [least] * (amount - 1), total - largest - least * (amount - 1)
    while rest > 0:
        candidates = [i for i in range(1, amount) if given[i] < largest] or [i for i in range(1, amount) if given[i] < bound]
        whole, remaining = sum([loads[i] for i in candidates]), rest
        for i in candidates:
            extra = min(bound - given[i], max(1, remaining * loads[i] // whole), rest)
            given[i] = given[i] + extra
            rest = rest - extra
    return np.array(given)


def bell_draw(own_key, extent, spread, reach, shards=(), kind=jnp.bfloat16):
    loudness = shard_levels(own_key, extent, shards, -0.22, 0.18) if shards else 1.0
    array = jax.random.normal(own_key, extent, jnp.float32) * spread * loudness
    return jnp.minimum(jnp.maximum(array, -reach), reach).astype(kind)


def setup_inputs(seed: int = 0) -> dict:
    key_of = jax.random.split(jax.random.key(seed), 6)
    queries = bell_draw(key_of[0], (QUERIES, LAT), 1.0, 6.0, ((0, 32),))
    cluster_keys = jax.random.split(jax.random.fold_in(key_of[1], 1), QUERIES // Q_DEV)
    cluster_turns = jax.random.permutation(jax.random.fold_in(key_of[1], 3), QUERIES // Q_DEV)
    cluster = jax.vmap(lambda own, number: routed_block(jax.random.fold_in(key_of[1], 2), own, number, Q_DEV, NB, 1, CAPB, 2))(cluster_keys, cluster_turns).reshape((QUERIES, 1))
    anchor_latent = bell_draw(key_of[2], (ANCHORS, LAT), 1.0, 6.0, ((0, 32),))
    anchor_labels = bell_draw(key_of[3], (ANCHORS, LABELS), 1.0, 6.0, ((0, 32), (1, 4)))
    tile_list = draw_tile_list(jax.random.fold_in(key_of[5], 71), 0)
    return dict(queries=queries, cluster=cluster, anchor_latent=anchor_latent, anchor_labels=anchor_labels, tile_list=tile_list)


kernel_width = 0.025
norm_epsilon = 1e-05

def unit_rows(values):
    widened = values.astype(jnp.float32)
    scaled = widened * lax.rsqrt(lax.optimization_barrier(jnp.mean(widened * widened, axis=-1, keepdims=True)) + norm_epsilon)
    return scaled.astype(jnp.bfloat16)

def transfer_block(row_block, latent_keys, label_values):
    similarity = jnp.einsum('rl,al->ra', row_block, latent_keys, preferred_element_type=jnp.float32) / latent_keys.shape[1]
    kernel = jnp.exp(similarity / kernel_width)
    totals = lax.optimization_barrier(jnp.sum(kernel, axis=1, keepdims=True))
    weighted = jnp.dot(kernel.astype(jnp.bfloat16), label_values, preferred_element_type=jnp.float32)
    return (weighted / totals).astype(jnp.bfloat16)

def reference(queries, cluster, anchor_latent, anchor_labels, tile_list):
    normed = unit_rows(queries)
    anchor_normed = unit_rows(anchor_latent).reshape(NTILES, TILE, LAT)
    label_tiles = anchor_labels.reshape(NTILES, TILE, LABELS)
    block_ids = cluster[:, 0].astype(jnp.int32)
    ordering = jnp.argsort(block_ids, stable=True).astype(jnp.int32)
    counts = lax.optimization_barrier(jnp.sum((block_ids[None, :] == jnp.arange(NB, dtype=jnp.int32)[:, None]).astype(jnp.int32), axis=1))
    starts = (jnp.cumsum(counts) - counts).astype(jnp.int32)

    def one_block(block_no):
        offsets = jnp.arange(ROWS_BLK, dtype=jnp.int32)
        position = jnp.minimum(starts[block_no] + offsets, QUERIES - 1).astype(jnp.int32)
        members = jnp.where(offsets < counts[block_no], ordering[position], QUERIES).astype(jnp.int32)
        row_block = normed[jnp.minimum(members, QUERIES - 1)]
        chosen = tile_list[block_no]
        key_rows = anchor_normed[chosen].reshape(TPB * TILE, LAT)
        values = label_tiles[chosen].reshape(TPB * TILE, LABELS)
        return (members, transfer_block(row_block, key_rows, values))
    members, blocks_out = lax.map(one_block, jnp.arange(NB, dtype=jnp.int32))
    result = jnp.zeros((QUERIES, LABELS), jnp.bfloat16)
    result = result.at[members.reshape(-1)].set(blocks_out.reshape(-1, LABELS), mode='drop')
    return result
```

```python
import functools
import jax
import jax.numpy as jnp
from jax import lax
from jax.sharding import PartitionSpec as P
from jax.experimental import pallas as pl
from jax.experimental.pallas import tpu as pltpu

TILE = 128
kernel_width = 0.025
norm_epsilon = 1e-05
PLANES = 4
LOG2E = 1.4426950408889634
VMEM = pl.BlockSpec(memory_space=pltpu.VMEM)
ANY = pl.BlockSpec(memory_space=pl.ANY)
SMEM = pl.BlockSpec(memory_space=pltpu.SMEM)


def unit_rows(values):
    widened = values.astype(jnp.float32)
    scaled = widened * lax.rsqrt(jnp.mean(widened * widened, axis=-1, keepdims=True) + norm_epsilon)
    return scaled.astype(jnp.bfloat16)


def params(**kw):
    return pltpu.CompilerParams(vmem_limit_bytes=56 * 1024 * 1024, **kw)


def rank_kernel(blocks, part, half, y_ref, ids_ref, inv_ref, pos_ref):
    y = y_ref[0]
    count = ids_ref.shape[1]
    step = 256
    upper = (
        lax.broadcasted_iota(jnp.int32, (step, step), 0)
        <= lax.broadcasted_iota(jnp.int32, (step, step), 1)
    ).astype(jnp.bfloat16)
    block_no = lax.broadcasted_iota(jnp.int32, (blocks, step), 0)
    slot_no = lax.broadcasted_iota(jnp.int32, (part, step), 0) + part * y
    lane = lax.broadcasted_iota(jnp.int32, (1, step), 1)
    carry = jnp.zeros((blocks, 1), jnp.float32)
    high = jnp.zeros((blocks, part), jnp.float32)
    low = jnp.zeros((blocks, part), jnp.float32)
    nt = (((1,), (1,)), ((), ()))
    for c in range(count // step):
        ids = ids_ref[:, c * step : (c + 1) * step]
        hit = block_no == ids
        hits = hit.astype(jnp.bfloat16)
        upto = jnp.dot(hits, upper, preferred_element_type=jnp.float32)
        rank = jnp.sum(jnp.where(hit, upto + carry, 0.0), axis=0, keepdims=True)
        rank = rank.astype(jnp.int32) - 1
        carry = carry + upto[:, step - 1 : step]
        turn = (y + PLANES - rank // part) % PLANES
        place = jnp.where(turn < 2, turn, 5 - turn)
        pos_ref[:, c * step : (c + 1) * step] = (
            place // 2 * half + ids // 2 * (4 * part) + place % 2 * (2 * part) + ids % 2 * part + rank % part
        )
        row = lane + c * step
        chosen = (slot_no == rank).astype(jnp.bfloat16)
        row_high = (row // 64).astype(jnp.float32)
        row_low = (row % 64).astype(jnp.float32)
        high += lax.dot_general(
            jnp.where(hit, row_high, 0.0).astype(jnp.bfloat16), chosen, nt, preferred_element_type=jnp.float32
        )
        low += lax.dot_general(
            jnp.where(hit, row_low, 0.0).astype(jnp.bfloat16), chosen, nt, preferred_element_type=jnp.float32
        )
    inv_ref[...] = high.astype(jnp.int32) * 64 + low.astype(jnp.int32)


def pack_kernel(inv_ref, x_ref, out_ref, rows, packed):
    count = x_ref.shape[0]
    lanes = 128
    step = 256

    @pl.loop(0, count // step)
    def _(c):
        at = pl.ds(pl.multiple_of(c * step, step), step)
        v = x_ref[at, :].astype(jnp.float32)
        v = v * lax.rsqrt(jnp.mean(v * v, axis=-1, keepdims=True) + norm_epsilon)
        rows[at, 0, :] = v[:, :lanes]
        rows[at, 1, :] = v[:, lanes:]

    blocks, part = inv_ref.shape

    @pl.loop(0, blocks)
    def _(b):
        for r in range(part):
            packed[b * part + r] = rows[inv_ref[b, r]]

    @pl.loop(0, blocks * part // step)
    def _(c):
        at = pl.ds(pl.multiple_of(c * step, step), step)
        out_ref[at, :lanes] = packed[at, 0, :].astype(jnp.bfloat16)
        out_ref[at, lanes:] = packed[at, 1, :].astype(jnp.bfloat16)


def tiles_kernel(asked_ref, tiles_ref, out_ref, sem):
    dests, slots = asked_ref.shape
    for d in range(dests):
        for s in range(slots):
            pltpu.make_async_copy(tiles_ref.at[asked_ref[d, s]], out_ref.at[d, s], sem).start()
    pltpu.make_async_copy(out_ref, out_ref, sem).wait()


def similar_kernel(scale, q_ref, k0_ref, k1_ref, k3_ref, k2a_ref, k2b_ref, out_ref, total_ref):
    block = pl.program_id(0)
    sources, part, width = q_ref.shape
    q = q_ref[...].reshape(sources * part, width)
    keys = k0_ref.shape[0]
    nt = (((1,), (1,)), ((), ()))
    total = jnp.zeros((sources * part, 1), jnp.float32)
    k2 = jnp.where(block == 0, k2a_ref[...], k2b_ref[...])
    for at, k in enumerate((k0_ref[...], k1_ref[...], k2, k3_ref[...])):
        s = lax.dot_general(q, k, nt, preferred_element_type=jnp.float32)
        e = jnp.exp2(s * scale)
        total = total + jnp.sum(e, axis=1, keepdims=True)
        out_ref[0, :, at * keys : (at + 1) * keys] = e.astype(jnp.bfloat16)
    total_ref[0] = jnp.broadcast_to(1.0 / total, total_ref.shape[1:])


def weigh_kernel(y_ref, slot_ref, ka_ref, kb_ref, ta_ref, tb_ref, got_ref, out_ref, values):
    block = pl.program_id(0)
    y = y_ref[0]
    tiles = slot_ref.shape[1]
    part = TILE // PLANES
    for turn in range(PLANES):
        row = pl.multiple_of((y + PLANES - turn) % PLANES * part, part)
        for j in range(tiles):
            at = (turn * tiles + j) * part
            values[at : at + part, :] = got_ref[slot_ref[block, j], pl.ds(row, part), :]
    sources = out_ref.shape[0]
    for p, (k_ref, t_ref) in enumerate(((ka_ref, ta_ref), (kb_ref, tb_ref))):
        w = jnp.dot(k_ref[0], values[...], preferred_element_type=jnp.float32)
        w = (w * t_ref[0][:, :1]).astype(jnp.bfloat16).reshape(sources, part, w.shape[1])
        at = pl.multiple_of((2 * p + block) * part, part)
        out_ref[:, pl.ds(at, part), :] = w


def unpack_kernel(pos_ref, a_ref, b_ref, out_ref, table, rows):
    lanes = 128
    step = 256
    half = a_ref.shape[0]
    for n, ref in enumerate((a_ref, b_ref)):

        @pl.loop(0, half // step)
        def _(c):
            at = pl.ds(pl.multiple_of(c * step, step), step)
            to = pl.ds(pl.multiple_of(c * step + n * half, step), step)
            v = ref[at, :].astype(jnp.float32)
            table[to, 0, :] = v[:, :lanes]
            table[to, 1, :] = v[:, lanes:]

    count = out_ref.shape[0]

    @pl.loop(0, count // 32)
    def _(c):
        for r in range(32):
            i = c * 32 + r
            rows[i] = table[pos_ref[0, i]]

    @pl.loop(0, count // step)
    def _(c):
        at = pl.ds(pl.multiple_of(c * step, step), step)
        out_ref[at, :lanes] = rows[at, 0, :].astype(jnp.bfloat16)
        out_ref[at, lanes:] = rows[at, 1, :].astype(jnp.bfloat16)


def shards(queries, cluster, anchor_latent, anchor_labels, tile_list):
    dp_count = lax.axis_size("dp")
    y = lax.axis_index("label").astype(jnp.int32)
    y1 = y.reshape(1)
    query_count, width = queries.shape
    blocks_here, tiles_each = tile_list.shape
    blocks = blocks_here * dp_count
    capacity = 2 * query_count // blocks
    part = capacity // PLANES
    tiles_here = anchor_latent.shape[0] // TILE
    tile_part = TILE // PLANES
    columns = anchor_labels.shape[1]
    wanted_count = blocks_here * tiles_each
    slots = 2
    half = dp_count * blocks_here * capacity // 2

    wanted = tile_list.reshape(wanted_count)
    source = wanted // tiles_here
    number = jnp.arange(wanted_count, dtype=jnp.int32)
    order = jnp.sum(
        ((source[:, None] == source[None, :]) & (number[None, :] < number[:, None])).astype(jnp.int32), axis=1
    )
    slot_of = source * slots + order
    asking = jnp.sum(
        jnp.where(
            slot_of[None, :] == jnp.arange(dp_count * slots, dtype=jnp.int32)[:, None], (wanted % tiles_here)[None, :], 0
        ),
        axis=1,
    ).reshape(dp_count, slots)
    asked = lax.all_to_all(asking, "dp", split_axis=0, concat_axis=0, tiled=True)
    slot_table = slot_of.reshape(blocks_here, tiles_each)

    inv, pos = pl.pallas_call(
        functools.partial(rank_kernel, blocks, part, half),
        in_specs=[SMEM, VMEM],
        out_specs=[VMEM, VMEM],
        out_shape=[
            jax.ShapeDtypeStruct((blocks, part), jnp.int32),
            jax.ShapeDtypeStruct((1, query_count), jnp.int32),
        ],
        compiler_params=params(),
        name="rank",
    )(y1, cluster.reshape(1, query_count))
    packed = pl.pallas_call(
        pack_kernel,
        in_specs=[SMEM, VMEM],
        out_specs=VMEM,
        out_shape=jax.ShapeDtypeStruct((blocks * part, width), jnp.bfloat16),
        scratch_shapes=[
            pltpu.VMEM((query_count, 2, 128), jnp.float32),
            pltpu.VMEM((blocks * part, 2, 128), jnp.float32),
        ],
        compiler_params=params(),
        name="pack",
    )(inv, queries)

    quarter = lax.dynamic_slice_in_dim(anchor_latent.reshape(tiles_here, TILE, width), y * tile_part, tile_part, axis=1)
    latent_out = unit_rows(quarter)[asked].reshape(dp_count, slots * tile_part, width)
    sent = jnp.concatenate([packed.reshape(dp_count, blocks_here * part, width), latent_out], axis=1)
    arrived = lax.all_to_all(sent, "dp", split_axis=0, concat_axis=0, tiled=True)

    label_out = pl.pallas_call(
        tiles_kernel,
        in_specs=[SMEM, VMEM],
        out_specs=ANY,
        out_shape=jax.ShapeDtypeStruct((dp_count, slots, TILE, columns), jnp.bfloat16),
        scratch_shapes=[pltpu.SemaphoreType.DMA],
        compiler_params=params(),
        name="label_tiles",
    )(asked, anchor_labels.reshape(tiles_here, TILE, columns))
    got_labels = lax.all_to_all(label_out, "dp", split_axis=0, concat_axis=0, tiled=True)
    got_labels = got_labels.reshape(dp_count * slots, TILE, columns)

    def shift(v, by):
        return lax.ppermute(v, "label", [(i, (i + by) % PLANES) for i in range(PLANES)])

    k0 = arrived[:, blocks_here * part :].reshape(dp_count * slots, tile_part, width)[slot_of]
    k1, k3 = shift(k0, 1), shift(k0, 3)
    k2a, k2b = shift(k1[:tiles_each], 1), shift(k3[tiles_each:], 3)
    q0 = arrived[:, : blocks_here * part]
    q1, q3 = shift(q0, 1), shift(q0, 3)
    mid = dp_count // 2
    q2 = jnp.concatenate([shift(q1[:mid], 1), shift(q3[mid:], 3)], axis=0)

    rows = dp_count * part
    keys = tiles_each * tile_part

    def similar(q):
        flat = blocks_here * keys
        return pl.pallas_call(
            functools.partial(similar_kernel, LOG2E / (width * kernel_width)),
            grid=(blocks_here,),
            in_specs=[pl.BlockSpec((dp_count, part, width), lambda b: (0, b, 0))]
            + [pl.BlockSpec((keys, width), lambda b: (b, 0))] * 3
            + [pl.BlockSpec((keys, width), lambda b: (0, 0))] * 2,
            out_specs=[
                pl.BlockSpec((1, rows, PLANES * keys), lambda b: (b, 0, 0)),
                pl.BlockSpec((1, rows, 128), lambda b: (b, 0, 0)),
            ],
            out_shape=[
                jax.ShapeDtypeStruct((blocks_here, rows, PLANES * keys), jnp.bfloat16),
                jax.ShapeDtypeStruct((blocks_here, rows, 128), jnp.float32),
            ],
            compiler_params=params(),
            cost_estimate=pl.CostEstimate(
                flops=2 * blocks_here * rows * PLANES * keys * width,
                transcendentals=blocks_here * rows * PLANES * keys,
                bytes_accessed=2 * blocks_here * rows * PLANES * keys,
            ),
            name="similar",
        )(q, k0.reshape(flat, width), k1.reshape(flat, width), k3.reshape(flat, width),
          k2a.reshape(keys, width), k2b.reshape(keys, width))

    def weigh(a, b):
        big = pl.BlockSpec((1, rows, PLANES * keys), lambda n: (n, 0, 0))
        tot = pl.BlockSpec((1, rows, 128), lambda n: (n, 0, 0))
        return pl.pallas_call(
            weigh_kernel,
            grid=(blocks_here,),
            in_specs=[SMEM, SMEM, big, big, tot, tot, VMEM],
            out_specs=pl.BlockSpec((dp_count, 2 * blocks_here * part, columns), lambda n: (0, 0, 0)),
            out_shape=jax.ShapeDtypeStruct((dp_count, 2 * blocks_here * part, columns), jnp.bfloat16),
            scratch_shapes=[pltpu.VMEM((tiles_each * TILE, columns), jnp.bfloat16)],
            compiler_params=params(),
            cost_estimate=pl.CostEstimate(
                flops=4 * blocks_here * rows * PLANES * keys * columns,
                transcendentals=0,
                bytes_accessed=4 * blocks_here * rows * PLANES * keys,
            ),
            name="weigh",
        )(y1, slot_table, a[0], b[0], a[1], b[1], got_labels)

    s0, s1, s3, s2 = similar(q0), similar(q1), similar(q3), similar(q2)
    back0 = lax.all_to_all(weigh(s0, s1), "dp", split_axis=0, concat_axis=0, tiled=True)
    back1 = lax.all_to_all(weigh(s3, s2), "dp", split_axis=0, concat_axis=0, tiled=True)
    return pl.pallas_call(
        unpack_kernel,
        in_specs=[SMEM, VMEM, VMEM],
        out_specs=VMEM,
        out_shape=jax.ShapeDtypeStruct((query_count, columns), jnp.bfloat16),
        scratch_shapes=[
            pltpu.VMEM((2 * half, 2, 128), jnp.float32),
            pltpu.VMEM((query_count, 2, 128), jnp.float32),
        ],
        compiler_params=params(),
        name="unpack",
    )(pos, back0.reshape(half, columns), back1.reshape(half, columns))


def solution(mesh):
    placed = (P("dp", None), P("dp", None), P("dp", None), P("dp", "label"), P("dp", None))
    return jax.shard_map(
        shards, mesh=mesh, in_specs=placed, out_specs=P("dp", "label"), check_vma=False
    )
```

```python
import functools
import jax
import jax.numpy as jnp
from jax import lax
from jax.sharding import PartitionSpec as P
from jax.experimental import pallas as pl
from jax.experimental.pallas import tpu as pltpu

TILE = 128
kernel_width = 0.025
norm_epsilon = 1e-05
PLANES = 4
LOG2E = 1.4426950408889634
VMEM = pl.BlockSpec(memory_space=pltpu.VMEM)
ANY = pl.BlockSpec(memory_space=pl.ANY)
SMEM = pl.BlockSpec(memory_space=pltpu.SMEM)


def unit_rows(values):
    widened = values.astype(jnp.float32)
    scaled = widened * lax.rsqrt(jnp.mean(widened * widened, axis=-1, keepdims=True) + norm_epsilon)
    return scaled.astype(jnp.bfloat16)


def params(mib, **kw):
    return pltpu.CompilerParams(vmem_limit_bytes=mib * 1024 * 1024, **kw)


def pack_kernel(
    blocks, part, tiles_here, y_ref, ids_ref, list_ref, x_ref,
    out_ref, pos_ref, rows, left, right, got_left, got_right, place, inv, row_sem, inv_sem,
):
    load = pltpu.make_async_copy(x_ref, rows, row_sem)
    load.start()
    y = y_ref[0]
    lanes = 128
    own = 2 * part
    wanted = list_ref[...]
    wanted = jnp.concatenate([wanted[n : n + 1] for n in range(wanted.shape[0])], axis=1)
    many = wanted.shape[1]
    across = lax.broadcasted_iota(jnp.int32, (many, many), 1)
    down = lax.broadcasted_iota(jnp.int32, (many, many), 0)
    source = wanted // tiles_here
    upright = jnp.sum(jnp.where(across == down, source.astype(jnp.float32), 0.0), axis=1, keepdims=True)
    same = (upright.astype(jnp.int32) == source) & (down < across)
    order = jnp.sum(same.astype(jnp.float32), axis=0, keepdims=True)
    holders, told_rows = out_ref.shape[0], out_ref.shape[1] - own
    holder = lax.broadcasted_iota(jnp.int32, (holders, many), 0) == source
    number = (wanted % tiles_here).astype(jnp.float32)
    for k in range(2):
        told = jnp.sum(jnp.where(holder & (order == k), number, 0.0), axis=1, keepdims=True)
        told = jnp.broadcast_to(told[:, :, None], (holders, told_rows, lanes))
        out_ref[:, own:, k * lanes : (k + 1) * lanes] = told.astype(jnp.bfloat16)

    count = ids_ref.shape[1]
    step = 256
    upper = (
        lax.broadcasted_iota(jnp.int32, (step, step), 0)
        <= lax.broadcasted_iota(jnp.int32, (step, step), 1)
    ).astype(jnp.bfloat16)
    block_no = lax.broadcasted_iota(jnp.int32, (blocks, step), 0)
    slot_no = lax.broadcasted_iota(jnp.int32, (lanes, step), 0) + part * y
    lane = lax.broadcasted_iota(jnp.int32, (1, step), 1)
    carry = jnp.zeros((blocks, 1), jnp.float32)
    high = jnp.zeros((blocks, lanes), jnp.float32)
    low = jnp.zeros((blocks, lanes), jnp.float32)
    nt = (((1,), (1,)), ((), ()))
    for c in range(count // step):
        ids = ids_ref[:, c * step : (c + 1) * step]
        hit = block_no == ids
        hits = hit.astype(jnp.bfloat16)
        upto = jnp.dot(hits, upper, preferred_element_type=jnp.float32)
        rank = jnp.sum(jnp.where(hit, upto + carry, 0.0), axis=0, keepdims=True)
        rank = rank.astype(jnp.int32) - 1
        carry = carry + upto[:, step - 1 : step]
        turn = (y + PLANES - rank // part) % PLANES
        piece = jnp.where(turn == 1, 0, jnp.where(turn == 3, 1, 2))
        within = ids % 2 * part + rank % part
        first = ids // 2 * (2 * part) + within
        later = blocks * part + ids // 2 * (6 * part) + piece * (2 * part) + within
        pos_ref[:, c * step : (c + 1) * step] = jnp.where(turn == 0, first, later)
        row = lane + c * step
        chosen = (slot_no == rank).astype(jnp.bfloat16)
        row_high = (row // 64).astype(jnp.float32)
        row_low = (row % 64).astype(jnp.float32)
        high += lax.dot_general(
            jnp.where(hit, row_high, 0.0).astype(jnp.bfloat16), chosen, nt, preferred_element_type=jnp.float32
        )
        low += lax.dot_general(
            jnp.where(hit, row_low, 0.0).astype(jnp.bfloat16), chosen, nt, preferred_element_type=jnp.float32
        )
    place[...] = high.astype(jnp.int32) * 64 + low.astype(jnp.int32)
    tell = pltpu.make_async_copy(place, inv, inv_sem)
    tell.start()
    load.wait()

    @pl.loop(0, count // step)
    def _(c):
        at = pl.ds(pl.multiple_of(c * step, step), step)
        left[at, :] = rows[at, :lanes].astype(jnp.float32)
        right[at, :] = rows[at, lanes:].astype(jnp.float32)

    tell.wait()

    @pl.loop(0, blocks)
    def _(b):
        at = pl.multiple_of(b * part, part)
        for r in range(part):
            i = inv[b, r]
            got_left[pl.ds(at + r, 1), :] = left[pl.ds(i, 1), :]
            got_right[pl.ds(at + r, 1), :] = right[pl.ds(i, 1), :]

    width = 2 * lanes
    some = 4

    @pl.loop(0, out_ref.shape[0] // some)
    def _(g):
        at = pl.ds(pl.multiple_of(g * some * own, some * own), some * own)
        a, b = got_left[at, :], got_right[at, :]
        scale = lax.rsqrt(jnp.sum(a * a + b * b, axis=-1, keepdims=True) / width + norm_epsilon)
        to = pl.ds(g * some, some)
        out_ref[to, :own, :lanes] = (a * scale).astype(jnp.bfloat16).reshape(some, own, lanes)
        out_ref[to, :own, lanes:] = (b * scale).astype(jnp.bfloat16).reshape(some, own, lanes)


def first_kernel(asked_ref, latent_ref, label_ref, out_ref, sem):
    dests, slots = asked_ref.shape
    part, rows = latent_ref.shape[1], label_ref.shape[1]
    for d in range(dests):
        for s in range(slots):
            pltpu.make_async_copy(
                latent_ref.at[asked_ref[d, s]], out_ref.at[d, pl.ds(s * part, part)], sem
            ).start()
        pltpu.make_async_copy(
            label_ref.at[asked_ref[d, 0]], out_ref.at[d, pl.ds(slots * part, rows)], sem
        ).start()
    pltpu.make_async_copy(out_ref, out_ref, sem).wait()


def second_kernel(asked_ref, label_ref, out_ref, sem):
    for d in range(asked_ref.shape[0]):
        pltpu.make_async_copy(label_ref.at[asked_ref[d, 1]], out_ref.at[d], sem).start()
    pltpu.make_async_copy(out_ref, out_ref, sem).wait()


def pick_kernel(slot_ref, arrived_ref, out_ref, sem):
    blocks, tiles = slot_ref.shape
    part = out_ref.shape[1]
    for n in range(blocks):
        for j in range(tiles):
            slot = slot_ref[n, j]
            row = pl.multiple_of(slot % 2 * part, part)
            pltpu.make_async_copy(
                arrived_ref.at[slot // 2, pl.ds(row, part)], out_ref.at[n * tiles + j], sem
            ).start()
    pltpu.make_async_copy(out_ref, out_ref, sem).wait()


def answer_kernel(scale, pieces, skip, y_ref, slot_ref, *refs):
    (k0_ref, k1_ref, k3_ref, k2a_ref, k2b_ref, first_ref, second_ref) = refs[-12:-5]
    out_ref, keys, values, key_sem, sems = refs[-5:]
    y = y_ref[0]
    blocks, tiles = slot_ref.shape
    rows = keys.shape[2]
    tile_part = rows // PLANES

    @pl.when((pl.program_id(0) == 0) & (pl.program_id(1) == 0))
    def _():
        for n in range(blocks):
            for turn, ref in enumerate((k0_ref, k1_ref, (k2a_ref, k2b_ref)[n], k3_ref)):
                row = pl.multiple_of((y + PLANES - turn) % PLANES * tile_part, tile_part)
                source = ref if turn == 2 else ref.at[pl.ds(n * tiles, tiles)]
                pltpu.make_async_copy(source, keys.at[n, :, pl.ds(row, tile_part)], key_sem.at[n]).start()
            for j in range(tiles):
                slot = slot_ref[n, j]
                to = values.at[n, pl.ds(j * rows, rows)]

                @pl.when(slot % 2 == 0)
                def _():
                    pltpu.make_async_copy(first_ref.at[slot // 2, pl.ds(skip, rows)], to, sems.at[n]).start()

                @pl.when(slot % 2 == 1)
                def _():
                    pltpu.make_async_copy(second_ref.at[slot // 2], to, sems.at[n]).start()

    block = pl.program_id(1)

    @pl.when(pl.program_id(0) == 0)
    def _():
        pltpu.make_async_copy(keys.at[block], keys.at[block], key_sem.at[block]).wait()

    nt = (((1,), (1,)), ((), ()))
    group = 4
    span = group * rows
    sources = out_ref.shape[0]
    for p in range(pieces):
        if p < 2:
            q = refs[p][...]
        else:
            q = jnp.where(pl.program_id(0) == 0, refs[2][...], refs[3][...])
        part, width = q.shape[1:]
        q = q.reshape(sources * part, width)
        total = jnp.zeros((sources * part, 1), jnp.float32)
        weighted = jnp.zeros((sources * part, values.shape[2]), jnp.float32)
        for at in range(tiles // group):
            k = keys[block, at * group : (at + 1) * group].reshape(span, width)
            s = lax.dot_general(q, k, nt, preferred_element_type=jnp.float32)
            e = jnp.exp2(s * scale)
            total = total + jnp.sum(e, axis=1, keepdims=True)
            if p == 0 and at == 0:

                @pl.when(pl.program_id(0) == 0)
                def _():
                    pltpu.make_async_copy(values.at[block], values.at[block], sems.at[block]).wait()

            weighted = weighted + jnp.dot(
                e.astype(jnp.bfloat16), values[block, at * span : (at + 1) * span], preferred_element_type=jnp.float32
            )
        answer = (weighted / total).astype(jnp.bfloat16).reshape(sources, part, values.shape[2])
        at = pl.multiple_of((2 * p + block) * part, part)
        out_ref[:, pl.ds(at, part), :] = answer


def unpack_kernel(pos_ref, a_ref, b_ref, out_ref, left, right, got_left, got_right):
    lanes = 128
    step = 256
    start = 0
    for ref in (a_ref, b_ref):

        @pl.loop(0, ref.shape[0] // step)
        def _(c):
            at = pl.ds(pl.multiple_of(c * step, step), step)
            to = pl.ds(pl.multiple_of(c * step + start, step), step)
            left[to, :] = ref[at, :lanes].astype(jnp.float32)
            right[to, :] = ref[at, lanes:].astype(jnp.float32)

        start += ref.shape[0]

    count = out_ref.shape[0]

    @pl.loop(0, count // 32)
    def _(c):
        at = pl.multiple_of(c * 32, 32)
        for r in range(32):
            i = pos_ref[0, at + r]
            got_left[pl.ds(at + r, 1), :] = left[pl.ds(i, 1), :]
            got_right[pl.ds(at + r, 1), :] = right[pl.ds(i, 1), :]

    @pl.loop(0, count // step)
    def _(c):
        at = pl.ds(pl.multiple_of(c * step, step), step)
        out_ref[at, :lanes] = got_left[at, :].astype(jnp.bfloat16)
        out_ref[at, lanes:] = got_right[at, :].astype(jnp.bfloat16)


def shards(queries, cluster, anchor_latent, anchor_labels, tile_list):
    dp_count = lax.axis_size("dp")
    y = lax.axis_index("label").astype(jnp.int32)
    y1 = y.reshape(1)
    query_count, width = queries.shape
    blocks_here, tiles_each = tile_list.shape
    blocks = blocks_here * dp_count
    capacity = 2 * query_count // blocks
    part = capacity // PLANES
    tiles_here = anchor_latent.shape[0] // TILE
    tile_part = TILE // PLANES
    columns = anchor_labels.shape[1]
    wanted_count = blocks_here * tiles_each
    slots = 2

    wanted = tile_list.reshape(wanted_count)
    source = wanted // tiles_here
    number = jnp.arange(wanted_count, dtype=jnp.int32)
    order = jnp.sum(
        ((source[:, None] == source[None, :]) & (number[None, :] < number[:, None])).astype(jnp.int32), axis=1
    )
    slot_of = source * slots + order
    slot_table = slot_of.reshape(blocks_here, tiles_each)

    own = blocks_here * part
    sent, pos = pl.pallas_call(
        functools.partial(pack_kernel, blocks, part, tiles_here),
        in_specs=[SMEM, VMEM, VMEM, ANY],
        out_specs=[VMEM, VMEM],
        out_shape=[
            jax.ShapeDtypeStruct((dp_count, own + 8, width), jnp.bfloat16),
            jax.ShapeDtypeStruct((1, query_count), jnp.int32),
        ],
        scratch_shapes=[
            pltpu.VMEM((query_count, width), jnp.bfloat16),
            pltpu.VMEM((query_count, 128), jnp.float32),
            pltpu.VMEM((query_count, 128), jnp.float32),
            pltpu.VMEM((blocks * part, 128), jnp.float32),
            pltpu.VMEM((blocks * part, 128), jnp.float32),
            pltpu.VMEM((blocks, 128), jnp.int32),
            pltpu.SMEM((blocks, 128), jnp.int32),
            pltpu.SemaphoreType.DMA,
            pltpu.SemaphoreType.DMA,
        ],
        compiler_params=params(60),
        name="pack",
    )(y1, cluster.reshape(1, query_count), tile_list, queries)
    arrived = lax.all_to_all(sent, "dp", split_axis=0, concat_axis=0, tiled=True)
    asked = arrived[:, own, :: width // slots].astype(jnp.int32)

    quarter = lax.dynamic_slice_in_dim(anchor_latent.reshape(tiles_here, TILE, width), y * tile_part, tile_part, axis=1)
    label_tiles = anchor_labels.reshape(tiles_here, TILE, columns)
    skip = slots * tile_part
    first_out = pl.pallas_call(
        first_kernel,
        in_specs=[SMEM, VMEM, VMEM],
        out_specs=ANY,
        out_shape=jax.ShapeDtypeStruct((dp_count, skip + TILE, columns), jnp.bfloat16),
        scratch_shapes=[pltpu.SemaphoreType.DMA],
        compiler_params=params(60),
        name="first_tiles",
    )(asked, unit_rows(quarter), label_tiles)
    got_first = lax.all_to_all(first_out, "dp", split_axis=0, concat_axis=0, tiled=True)
    second_out = pl.pallas_call(
        second_kernel,
        in_specs=[SMEM, VMEM],
        out_specs=ANY,
        out_shape=jax.ShapeDtypeStruct((dp_count, TILE, columns), jnp.bfloat16),
        scratch_shapes=[pltpu.SemaphoreType.DMA],
        compiler_params=params(60),
        name="second_tiles",
    )(asked, label_tiles)

    def shift(v, by):
        return lax.ppermute(v, "label", [(i, (i + by) % PLANES) for i in range(PLANES)])

    q0 = arrived[:, :own]
    q1, q3 = shift(q0, 1), shift(q0, 3)
    mid = dp_count // 2
    q2a, q2b = shift(q1[:mid], 1), shift(q3[mid:], 3)
    second_out = lax.optimization_barrier((second_out, q1, q3))[0]
    got_second = lax.all_to_all(second_out, "dp", split_axis=0, concat_axis=0, tiled=True)
    k0 = pl.pallas_call(
        pick_kernel,
        in_specs=[SMEM, ANY],
        out_specs=VMEM,
        out_shape=jax.ShapeDtypeStruct((wanted_count, tile_part, width), jnp.bfloat16),
        scratch_shapes=[pltpu.SemaphoreType.DMA],
        compiler_params=params(60),
        name="pick",
    )(slot_table, got_first)
    k1, k3 = shift(k0, 1), shift(k0, 3)
    k2a, k2b = shift(k1[:tiles_each], 1), shift(k3[tiles_each:], 3)

    rows = dp_count * part
    keys = tiles_each * TILE
    cuts = 2

    def answers(pieces, *pieces_in):
        piece = pl.BlockSpec((dp_count // cuts, part, width), lambda r, n: (r, n, 0))
        half = pl.BlockSpec((dp_count // cuts, part, width), lambda r, n: (0, n, 0))
        specs = [piece] if pieces == 1 else [piece, piece, half, half]
        answer = pieces * own
        return pl.pallas_call(
            functools.partial(answer_kernel, LOG2E / (width * kernel_width), pieces, skip),
            grid=(cuts, blocks_here),
            in_specs=[SMEM, SMEM] + specs + [ANY] * 7,
            out_specs=pl.BlockSpec((dp_count // cuts, answer, columns), lambda r, n: (r, 0, 0)),
            out_shape=jax.ShapeDtypeStruct((dp_count, answer, columns), jnp.bfloat16),
            scratch_shapes=[
                pltpu.VMEM((blocks_here, tiles_each, TILE, width), jnp.bfloat16),
                pltpu.VMEM((blocks_here, keys, columns), jnp.bfloat16),
                pltpu.SemaphoreType.DMA((blocks_here,)),
                pltpu.SemaphoreType.DMA((blocks_here,)),
            ],
            compiler_params=params(60),
            cost_estimate=pl.CostEstimate(
                flops=2 * pieces * blocks_here * rows * keys * (width + columns),
                transcendentals=pieces * blocks_here * rows * keys,
                bytes_accessed=2 * blocks_here * keys * (width + columns),
            ),
            name="answers",
        )(y1, slot_table, *pieces_in, k0, k1, k3, k2a, k2b, got_first, got_second)

    first = answers(1, arrived)
    back0 = lax.all_to_all(first, "dp", split_axis=0, concat_axis=0, tiled=True)
    rest = answers(3, *lax.optimization_barrier((q1, q3, q2a, q2b, first))[:4])
    back1 = lax.all_to_all(rest, "dp", split_axis=0, concat_axis=0, tiled=True)
    count0, count1 = (back.shape[0] * back.shape[1] for back in (back0, back1))
    return pl.pallas_call(
        unpack_kernel,
        in_specs=[SMEM, VMEM, VMEM],
        out_specs=VMEM,
        out_shape=jax.ShapeDtypeStruct((query_count, columns), jnp.bfloat16),
        scratch_shapes=[
            pltpu.VMEM((count0 + count1, 128), jnp.float32),
            pltpu.VMEM((count0 + count1, 128), jnp.float32),
            pltpu.VMEM((query_count, 128), jnp.float32),
            pltpu.VMEM((query_count, 128), jnp.float32),
        ],
        compiler_params=params(60),
        name="unpack",
    )(pos, back0.reshape(count0, columns), back1.reshape(count1, columns))


def solution(mesh):
    placed = (P("dp", None), P("dp", None), P("dp", None), P("dp", "label"), P("dp", None))
    return jax.shard_map(
        shards, mesh=mesh, in_specs=placed, out_specs=P("dp", "label"), check_vma=False
    )
```

```python
import functools
import jax
import jax.numpy as jnp
from jax import lax
from jax.sharding import PartitionSpec as P
from jax.experimental import pallas as pl
from jax.experimental.pallas import tpu as pltpu

TILE = 128
kernel_width = 0.025
norm_epsilon = 1e-05
PLANES = 4
FULL = 64
LOG2E = 1.4426950408889634
VMEM = pl.BlockSpec(memory_space=pltpu.VMEM)
ANY = pl.BlockSpec(memory_space=pl.ANY)
SMEM = pl.BlockSpec(memory_space=pltpu.SMEM)


def unit_rows(values):
    widened = values.astype(jnp.float32)
    scaled = widened * lax.rsqrt(jnp.mean(widened * widened, axis=-1, keepdims=True) + norm_epsilon)
    return scaled.astype(jnp.bfloat16)


def params(mib, **kw):
    return pltpu.CompilerParams(vmem_limit_bytes=min(mib * 1024 * 1024, 67043328), **kw)


def pack_kernel(
    blocks, part, tiles_here, y_ref, ids_ref, list_ref, x_ref,
    out_ref, pos_ref, rows, table, got, hold, inv, row_sem, inv_sem,
):
    load = pltpu.make_async_copy(x_ref, rows, row_sem)
    load.start()
    y = y_ref[0]
    lanes = 128
    own = 2 * part
    wanted = list_ref[...]
    wanted = jnp.concatenate([wanted[n : n + 1] for n in range(wanted.shape[0])], axis=1)
    many = wanted.shape[1]
    across = lax.broadcasted_iota(jnp.int32, (many, many), 1)
    down = lax.broadcasted_iota(jnp.int32, (many, many), 0)
    source = wanted // tiles_here
    upright = jnp.sum(jnp.where(across == down, source.astype(jnp.float32), 0.0), axis=1, keepdims=True)
    same = (upright.astype(jnp.int32) == source) & (down < across)
    order = jnp.sum(same.astype(jnp.float32), axis=0, keepdims=True)
    holders, told_rows = out_ref.shape[0], out_ref.shape[1] - own
    holder = lax.broadcasted_iota(jnp.int32, (holders, many), 0) == source
    number = (wanted % tiles_here).astype(jnp.float32)
    for k in range(2):
        told = jnp.sum(jnp.where(holder & (order == k), number, 0.0), axis=1, keepdims=True)
        told = jnp.broadcast_to(told[:, :, None], (holders, told_rows, lanes))
        out_ref[:, own:, k * lanes : (k + 1) * lanes] = told.astype(jnp.bfloat16)

    count = ids_ref.shape[1]
    step = 256
    upper = (
        lax.broadcasted_iota(jnp.int32, (step, step), 0)
        <= lax.broadcasted_iota(jnp.int32, (step, step), 1)
    ).astype(jnp.bfloat16)
    block_no = lax.broadcasted_iota(jnp.int32, (blocks, step), 0)
    slot_no = lax.broadcasted_iota(jnp.int32, (lanes, step), 0) + part * y
    lane = lax.broadcasted_iota(jnp.int32, (1, step), 1)
    carry = jnp.zeros((blocks, 1), jnp.float32)
    high = jnp.zeros((blocks, lanes), jnp.float32)
    low = jnp.zeros((blocks, lanes), jnp.float32)
    nt = (((1,), (1,)), ((), ()))
    for c in range(count // step):
        ids = ids_ref[:, c * step : (c + 1) * step]
        hit = block_no == ids
        hits = hit.astype(jnp.bfloat16)
        upto = jnp.dot(hits, upper, preferred_element_type=jnp.float32)
        rank = jnp.sum(jnp.where(hit, upto + carry, 0.0), axis=0, keepdims=True)
        rank = rank.astype(jnp.int32) - 1
        carry = carry + upto[:, step - 1 : step]
        turn = (y + PLANES - rank // part) % PLANES
        place = jnp.where(turn < 2, turn, 5 - turn)
        pos_ref[:, c * step : (c + 1) * step] = 2 * (
            place // 2 * (2 * blocks * part)
            + ids // 2 * (4 * part)
            + place % 2 * (2 * part)
            + ids % 2 * part
            + rank % part
        )
        row = lane + c * step
        chosen = (slot_no == rank).astype(jnp.bfloat16)
        row_high = (row // 64).astype(jnp.float32)
        row_low = (row % 64).astype(jnp.float32)
        high += lax.dot_general(
            jnp.where(hit, row_high, 0.0).astype(jnp.bfloat16), chosen, nt, preferred_element_type=jnp.float32
        )
        low += lax.dot_general(
            jnp.where(hit, row_low, 0.0).astype(jnp.bfloat16), chosen, nt, preferred_element_type=jnp.float32
        )
    hold[...] = high.astype(jnp.int32) * 128 + low.astype(jnp.int32) * 2
    tell = pltpu.make_async_copy(hold, inv, inv_sem)
    tell.start()
    load.wait()

    @pl.loop(0, count // step)
    def _(c):
        at = pl.ds(pl.multiple_of(c * step, step), step)
        to = pl.multiple_of(2 * c * step, 2 * step)
        table[pl.ds(to, step, stride=2), :] = rows[at, :lanes].astype(jnp.float32)
        table[pl.ds(to + 1, step, stride=2), :] = rows[at, lanes:].astype(jnp.float32)

    tell.wait()

    @pl.loop(0, blocks)
    def _(b):
        at = pl.multiple_of(2 * b * part, 2 * part)
        for r in range(part):
            i = pl.multiple_of(inv[b, r], 2)
            got[pl.ds(at + 2 * r, 2), :] = table[pl.ds(i, 2), :]

    width = 2 * lanes
    some = 4

    @pl.loop(0, out_ref.shape[0] // some)
    def _(g):
        at = pl.multiple_of(2 * g * some * own, 2 * some * own)
        a = got[pl.ds(at, some * own, stride=2), :]
        b = got[pl.ds(at + 1, some * own, stride=2), :]
        scale = lax.rsqrt(jnp.sum(a * a + b * b, axis=-1, keepdims=True) / width + norm_epsilon)
        to = pl.ds(g * some, some)
        out_ref[to, :own, :lanes] = (a * scale).astype(jnp.bfloat16).reshape(some, own, lanes)
        out_ref[to, :own, lanes:] = (b * scale).astype(jnp.bfloat16).reshape(some, own, lanes)


def first_kernel(asked_ref, latent_ref, label_ref, out_ref, sem):
    dests, slots = asked_ref.shape
    part, rows = latent_ref.shape[1], label_ref.shape[1]
    for d in range(dests):
        for s in range(slots):
            pltpu.make_async_copy(
                latent_ref.at[asked_ref[d, s]], out_ref.at[d, pl.ds(s * part, part)], sem
            ).start()
        pltpu.make_async_copy(
            label_ref.at[asked_ref[d, 0]], out_ref.at[d, pl.ds(slots * part, rows)], sem
        ).start()
    pltpu.make_async_copy(out_ref, out_ref, sem).wait()


def second_kernel(asked_ref, label_ref, out_ref, sem):
    for d in range(asked_ref.shape[0]):
        pltpu.make_async_copy(label_ref.at[asked_ref[d, 1]], out_ref.at[d], sem).start()
    pltpu.make_async_copy(out_ref, out_ref, sem).wait()


def pick_kernel(slot_ref, arrived_ref, *refs):
    _, tiles = slot_ref.shape
    sem = refs[-1]
    part = refs[0].shape[1]
    for n, out_ref in enumerate(refs[:-1]):
        for j in range(tiles):
            slot = slot_ref[n, j]
            row = pl.multiple_of(slot % 2 * part, part)
            pltpu.make_async_copy(
                arrived_ref.at[slot // 2, pl.ds(row, part)], out_ref.at[j], sem.at[n]
            ).start()
    for n, out_ref in enumerate(refs[:-1]):
        pltpu.make_async_copy(out_ref, out_ref, sem.at[n]).wait()


def answer_kernel(scale, skip, y_ref, slot_ref, *refs):
    latents, (first_ref, second_ref) = refs[-15:-7], refs[-7:-5]
    out_ref, keys, values, key_sem, sems = refs[-5:]
    pieces = refs[:-15]
    y = y_ref[0]
    blocks, tiles = slot_ref.shape
    rows = keys.shape[2]
    tile_part = rows // PLANES
    piece, block = pl.program_id(0), pl.program_id(1)

    @pl.when((piece == 0) & (block == 0))
    def _():
        for n in range(blocks):
            for turn, ref in enumerate(latents[n * PLANES : (n + 1) * PLANES]):
                row = pl.multiple_of((y + PLANES - turn) % PLANES * tile_part, tile_part)
                pltpu.make_async_copy(ref, keys.at[n, :, pl.ds(row, tile_part)], key_sem.at[n]).start()

            @pl.loop(0, tiles)
            def _(j):
                slot = slot_ref[n, j]
                to = values.at[n, pl.ds(pl.multiple_of(j * rows, rows), rows)]

                @pl.when(slot % 2 == 0)
                def _():
                    pltpu.make_async_copy(first_ref.at[slot // 2, pl.ds(skip, rows)], to, sems.at[n]).start()

                @pl.when(slot % 2 == 1)
                def _():
                    pltpu.make_async_copy(second_ref.at[slot // 2], to, sems.at[n]).start()

    @pl.when(piece == 0)
    def _():
        pltpu.make_async_copy(keys.at[block], keys.at[block], key_sem.at[block]).wait()
        pltpu.make_async_copy(values.at[block], values.at[block], sems.at[block]).wait()

    nt = (((1,), (1,)), ((), ()))
    group = 2
    span = group * rows
    sources = out_ref.shape[0]
    second = pieces[1][...]
    if len(pieces) == 3:
        second = jnp.concatenate([second, pieces[2][...]], axis=0)
    q = jnp.where(piece == 0, pieces[0][...], second)
    part, width = q.shape[1:]
    q = q.reshape(sources * part, width)
    total = jnp.zeros((sources * part, 1), jnp.float32)
    weighted = jnp.zeros((sources * part, values.shape[2]), jnp.float32)
    for at in range(tiles // group):
        k = keys[block, at * group : (at + 1) * group].reshape(span, width)
        s = lax.dot_general(q, k, nt, preferred_element_type=jnp.float32)
        e = jnp.exp2(s * scale)
        total = total + jnp.sum(e, axis=1, keepdims=True)
        weighted = weighted + jnp.dot(
            e.astype(jnp.bfloat16), values[block, at * span : (at + 1) * span], preferred_element_type=jnp.float32
        )
    answer = (weighted / total).astype(jnp.bfloat16).reshape(sources, part, values.shape[2])
    at = pl.multiple_of((2 * piece + block) * part, part)
    out_ref[:, pl.ds(at, part), :] = answer


def unpack_kernel(pos_ref, a_ref, b_ref, out_ref, table, got):
    lanes = 128
    step = 256
    start = 0
    for ref in (a_ref, b_ref):

        @pl.loop(0, ref.shape[0] // step)
        def _(c):
            at = pl.ds(pl.multiple_of(c * step, step), step)
            to = pl.multiple_of(2 * (c * step + start), 2 * step)
            table[pl.ds(to, step, stride=2), :] = ref[at, :lanes].astype(jnp.float32)
            table[pl.ds(to + 1, step, stride=2), :] = ref[at, lanes:].astype(jnp.float32)

        start += ref.shape[0]

    count = out_ref.shape[0]

    @pl.loop(0, count // 32)
    def _(c):
        at = pl.multiple_of(c * 64, 64)
        for r in range(32):
            i = pl.multiple_of(pos_ref[0, c * 32 + r], 2)
            got[pl.ds(at + 2 * r, 2), :] = table[pl.ds(i, 2), :]

    @pl.loop(0, count // step)
    def _(c):
        at = pl.multiple_of(c * step, step)
        out_ref[pl.ds(at, step), :lanes] = got[pl.ds(2 * at, step, stride=2), :].astype(jnp.bfloat16)
        out_ref[pl.ds(at, step), lanes:] = got[pl.ds(2 * at + 1, step, stride=2), :].astype(jnp.bfloat16)


def shards(queries, cluster, anchor_latent, anchor_labels, tile_list):
    dp_count = lax.axis_size("dp")
    y = lax.axis_index("label").astype(jnp.int32)
    y1 = y.reshape(1)
    query_count, width = queries.shape
    blocks_here, tiles_each = tile_list.shape
    blocks = blocks_here * dp_count
    capacity = 2 * query_count // blocks
    part = capacity // PLANES
    tiles_here = anchor_latent.shape[0] // TILE
    tile_part = TILE // PLANES
    columns = anchor_labels.shape[1]
    wanted_count = blocks_here * tiles_each
    slots = 2

    wanted = tile_list.reshape(wanted_count)
    source = wanted // tiles_here
    number = jnp.arange(wanted_count, dtype=jnp.int32)
    order = jnp.sum(
        ((source[:, None] == source[None, :]) & (number[None, :] < number[:, None])).astype(jnp.int32), axis=1
    )
    slot_of = source * slots + order
    slot_table = slot_of.reshape(blocks_here, tiles_each)

    own = blocks_here * part
    sent, pos = pl.pallas_call(
        functools.partial(pack_kernel, blocks, part, tiles_here),
        in_specs=[SMEM, VMEM, VMEM, ANY],
        out_specs=[VMEM, VMEM],
        out_shape=[
            jax.ShapeDtypeStruct((dp_count, own + 8, width), jnp.bfloat16),
            jax.ShapeDtypeStruct((1, query_count), jnp.int32),
        ],
        scratch_shapes=[
            pltpu.VMEM((query_count, width), jnp.bfloat16),
            pltpu.VMEM((2 * query_count, 128), jnp.float32),
            pltpu.VMEM((2 * blocks * part, 128), jnp.float32),
            pltpu.VMEM((blocks, 128), jnp.int32),
            pltpu.SMEM((blocks, 128), jnp.int32),
            pltpu.SemaphoreType.DMA,
            pltpu.SemaphoreType.DMA,
        ],
        compiler_params=params(FULL),
        name="pack",
    )(y1, cluster.reshape(1, query_count), tile_list, queries)
    arrived = lax.all_to_all(sent, "dp", split_axis=0, concat_axis=0, tiled=True)
    asked = arrived[:, own, :: width // slots].astype(jnp.int32)

    quarter = lax.dynamic_slice_in_dim(anchor_latent.reshape(tiles_here, TILE, width), y * tile_part, tile_part, axis=1)
    label_tiles = anchor_labels.reshape(tiles_here, TILE, columns)
    skip = slots * tile_part
    first_out = pl.pallas_call(
        first_kernel,
        in_specs=[SMEM, VMEM, VMEM],
        out_specs=ANY,
        out_shape=jax.ShapeDtypeStruct((dp_count, skip + TILE, columns), jnp.bfloat16),
        scratch_shapes=[pltpu.SemaphoreType.DMA],
        compiler_params=params(8),
        name="first_tiles",
    )(asked, unit_rows(quarter), label_tiles)
    got_first = lax.all_to_all(first_out, "dp", split_axis=0, concat_axis=0, tiled=True)
    second_out = pl.pallas_call(
        second_kernel,
        in_specs=[SMEM, VMEM],
        out_specs=ANY,
        out_shape=jax.ShapeDtypeStruct((dp_count, TILE, columns), jnp.bfloat16),
        scratch_shapes=[pltpu.SemaphoreType.DMA],
        compiler_params=params(8),
        name="second_tiles",
    )(asked, label_tiles)

    def shift(v, by):
        return lax.ppermute(v, "label", [(i, (i + by) % PLANES) for i in range(PLANES)])

    q0 = arrived[:, :own]
    q1, q3 = shift(q0, 1), shift(q0, 3)
    mid = dp_count // 2
    q2a, q2b = shift(q1[:mid], 1), shift(q3[mid:], 3)
    second_out = lax.optimization_barrier((second_out, q1, q3))[0]
    got_second = lax.all_to_all(second_out, "dp", split_axis=0, concat_axis=0, tiled=True)
    k0 = pl.pallas_call(
        pick_kernel,
        in_specs=[SMEM, ANY],
        out_specs=[VMEM] * blocks_here,
        out_shape=[jax.ShapeDtypeStruct((tiles_each, tile_part, width), jnp.bfloat16)] * blocks_here,
        scratch_shapes=[pltpu.SemaphoreType.DMA((blocks_here,))],
        compiler_params=params(FULL),
        name="pick",
    )(slot_table, lax.optimization_barrier((got_first, q2a, q2b))[0])
    k1a, k3b = shift(k0[0], 1), shift(k0[1], 3)
    k1b, k3a = shift(k0[1], 1), shift(k0[0], 3)
    k2a, k2b = shift(k1a, 1), shift(k3b, 3)
    latents = [k0[0], k1a, k2a, k3a, k0[1], k1b, k2b, k3b]

    rows = dp_count * part
    keys = tiles_each * TILE

    def answers(*pieces):
        piece = pl.BlockSpec((dp_count, part, width), lambda p, n: (0, n, 0))
        half = pl.BlockSpec((mid, part, width), lambda p, n: (0, n, 0))
        specs = [piece, piece] if len(pieces) == 2 else [piece, half, half]
        return pl.pallas_call(
            functools.partial(answer_kernel, LOG2E / (width * kernel_width), skip),
            grid=(2, blocks_here),
            in_specs=[SMEM, SMEM] + specs + [ANY] * 10,
            out_specs=pl.BlockSpec((dp_count, 2 * own, columns), lambda p, n: (0, 0, 0)),
            out_shape=jax.ShapeDtypeStruct((dp_count, 2 * own, columns), jnp.bfloat16),
            scratch_shapes=[
                pltpu.VMEM((blocks_here, tiles_each, TILE, width), jnp.bfloat16),
                pltpu.VMEM((blocks_here, keys, columns), jnp.bfloat16),
                pltpu.SemaphoreType.DMA((blocks_here,)),
                pltpu.SemaphoreType.DMA((blocks_here,)),
            ],
            compiler_params=params(FULL),
            cost_estimate=pl.CostEstimate(
                flops=4 * blocks_here * rows * keys * (width + columns),
                transcendentals=2 * blocks_here * rows * keys,
                bytes_accessed=2 * blocks_here * keys * (width + columns),
            ),
            name="answers",
        )(y1, slot_table, *pieces, *latents, got_first, got_second)

    first = answers(arrived, q1)
    back0 = lax.all_to_all(first, "dp", split_axis=0, concat_axis=0, tiled=True)
    rest = answers(*lax.optimization_barrier((q3, q2a, q2b, first))[:3])
    back1 = lax.all_to_all(rest, "dp", split_axis=0, concat_axis=0, tiled=True)
    count0, count1 = (back.shape[0] * back.shape[1] for back in (back0, back1))
    return pl.pallas_call(
        unpack_kernel,
        in_specs=[SMEM, VMEM, VMEM],
        out_specs=VMEM,
        out_shape=jax.ShapeDtypeStruct((query_count, columns), jnp.bfloat16),
        scratch_shapes=[
            pltpu.VMEM((2 * (count0 + count1), 128), jnp.float32),
            pltpu.VMEM((2 * query_count, 128), jnp.float32),
        ],
        compiler_params=params(24),
        name="unpack",
    )(pos, back0.reshape(count0, columns), back1.reshape(count1, columns))


def solution(mesh):
    placed = (P("dp", None), P("dp", None), P("dp", None), P("dp", "label"), P("dp", None))
    return jax.shard_map(shards, mesh=mesh, in_specs=placed, out_specs=P("dp", "label"), check_vma=False)
```

```python
import functools
import jax
import jax.numpy as jnp
from jax import lax
from jax.sharding import PartitionSpec as P
from jax.experimental import pallas as pl
from jax.experimental.pallas import tpu as pltpu

TILE = 128
kernel_width = 0.025
norm_epsilon = 1e-05
PLANES = 4
FULL = 64
LOG2E = 1.4426950408889634
VMEM = pl.BlockSpec(memory_space=pltpu.VMEM)
ANY = pl.BlockSpec(memory_space=pl.ANY)
SMEM = pl.BlockSpec(memory_space=pltpu.SMEM)


def unit_rows(values):
    widened = values.astype(jnp.float32)
    scaled = widened * lax.rsqrt(jnp.mean(widened * widened, axis=-1, keepdims=True) + norm_epsilon)
    return scaled.astype(jnp.bfloat16)


def params(mib, **kw):
    return pltpu.CompilerParams(vmem_limit_bytes=min(mib * 1024 * 1024, 67043328), **kw)


def pack_kernel(
    blocks, part, tiles_here, y_ref, ids_ref, list_ref, x_ref,
    out_ref, pos_ref, rows, table, got, hold, inv, row_sem, inv_sem,
):
    load = pltpu.make_async_copy(x_ref, rows, row_sem)
    load.start()
    y = y_ref[0]
    lanes = 128
    own = 2 * part
    wanted = list_ref[...]
    wanted = jnp.concatenate([wanted[n : n + 1] for n in range(wanted.shape[0])], axis=1)
    many = wanted.shape[1]
    across = lax.broadcasted_iota(jnp.int32, (many, many), 1)
    down = lax.broadcasted_iota(jnp.int32, (many, many), 0)
    source = wanted // tiles_here
    upright = jnp.sum(jnp.where(across == down, source.astype(jnp.float32), 0.0), axis=1, keepdims=True)
    same = (upright.astype(jnp.int32) == source) & (down < across)
    order = jnp.sum(same.astype(jnp.float32), axis=0, keepdims=True)
    holders, told_rows = out_ref.shape[0], out_ref.shape[1] - own
    holder = lax.broadcasted_iota(jnp.int32, (holders, many), 0) == source
    number = (wanted % tiles_here).astype(jnp.float32)
    for k in range(2):
        told = jnp.sum(jnp.where(holder & (order == k), number, 0.0), axis=1, keepdims=True)
        told = jnp.broadcast_to(told[:, :, None], (holders, told_rows, lanes))
        out_ref[:, own:, k * lanes : (k + 1) * lanes] = told.astype(jnp.bfloat16)

    count = ids_ref.shape[1]
    step = 256
    upper = (
        lax.broadcasted_iota(jnp.int32, (step, step), 0)
        <= lax.broadcasted_iota(jnp.int32, (step, step), 1)
    ).astype(jnp.bfloat16)
    block_no = lax.broadcasted_iota(jnp.int32, (blocks, step), 0)
    slot_no = lax.broadcasted_iota(jnp.int32, (lanes, step), 0) + part * y
    lane = lax.broadcasted_iota(jnp.int32, (1, step), 1)
    carry = jnp.zeros((blocks, 1), jnp.float32)
    high = jnp.zeros((blocks, lanes), jnp.float32)
    low = jnp.zeros((blocks, lanes), jnp.float32)
    nt = (((1,), (1,)), ((), ()))
    for c in range(count // step):
        ids = ids_ref[:, c * step : (c + 1) * step]
        hit = block_no == ids
        hits = hit.astype(jnp.bfloat16)
        upto = jnp.dot(hits, upper, preferred_element_type=jnp.float32)
        rank = jnp.sum(jnp.where(hit, upto + carry, 0.0), axis=0, keepdims=True)
        rank = rank.astype(jnp.int32) - 1
        carry = carry + upto[:, step - 1 : step]
        turn = (y + PLANES - rank // part) % PLANES
        place = jnp.where(turn < 2, turn, 5 - turn)
        pos_ref[:, c * step : (c + 1) * step] = 2 * (
            ids // 2 * (2 * PLANES * part)
            + place * (2 * part)
            + ids % 2 * part
            + rank % part
        )
        row = lane + c * step
        chosen = (slot_no == rank).astype(jnp.bfloat16)
        row_high = (row // 64).astype(jnp.float32)
        row_low = (row % 64).astype(jnp.float32)
        high += lax.dot_general(
            jnp.where(hit, row_high, 0.0).astype(jnp.bfloat16), chosen, nt, preferred_element_type=jnp.float32
        )
        low += lax.dot_general(
            jnp.where(hit, row_low, 0.0).astype(jnp.bfloat16), chosen, nt, preferred_element_type=jnp.float32
        )
    hold[...] = high.astype(jnp.int32) * 128 + low.astype(jnp.int32) * 2
    tell = pltpu.make_async_copy(hold, inv, inv_sem)
    tell.start()
    load.wait()

    @pl.loop(0, count // step)
    def _(c):
        at = pl.ds(pl.multiple_of(c * step, step), step)
        to = pl.multiple_of(2 * c * step, 2 * step)
        table[pl.ds(to, step, stride=2), :] = rows[at, :lanes].astype(jnp.float32)
        table[pl.ds(to + 1, step, stride=2), :] = rows[at, lanes:].astype(jnp.float32)

    tell.wait()

    @pl.loop(0, blocks)
    def _(b):
        at = pl.multiple_of(2 * b * part, 2 * part)
        for r in range(part):
            i = pl.multiple_of(inv[b, r], 2)
            got[pl.ds(at + 2 * r, 2), :] = table[pl.ds(i, 2), :]

    width = 2 * lanes
    some = 4

    @pl.loop(0, out_ref.shape[0] // some)
    def _(g):
        at = pl.multiple_of(2 * g * some * own, 2 * some * own)
        a = got[pl.ds(at, some * own, stride=2), :]
        b = got[pl.ds(at + 1, some * own, stride=2), :]
        scale = lax.rsqrt(jnp.sum(a * a + b * b, axis=-1, keepdims=True) / width + norm_epsilon)
        to = pl.ds(g * some, some)
        out_ref[to, :own, :lanes] = (a * scale).astype(jnp.bfloat16).reshape(some, own, lanes)
        out_ref[to, :own, lanes:] = (b * scale).astype(jnp.bfloat16).reshape(some, own, lanes)


def slots_kernel(asked_ref, tile_ref, out_ref, sem):
    dests, slots = asked_ref.shape
    part = tile_ref.shape[1]
    for d in range(dests):
        for s in range(slots):
            pltpu.make_async_copy(tile_ref.at[asked_ref[d, s]], out_ref.at[d, pl.ds(s * part, part)], sem).start()
    pltpu.make_async_copy(out_ref, out_ref, sem).wait()


def one_slot_kernel(slot, asked_ref, tile_ref, out_ref, sem):
    for d in range(asked_ref.shape[0]):
        pltpu.make_async_copy(tile_ref.at[asked_ref[d, slot]], out_ref.at[d], sem).start()
    pltpu.make_async_copy(out_ref, out_ref, sem).wait()


def pick_kernel(slot_ref, arrived_ref, *refs):
    _, tiles = slot_ref.shape
    sem = refs[-1]
    part = refs[0].shape[1]
    for n, out_ref in enumerate(refs[:-1]):
        for j in range(tiles):
            slot = slot_ref[n, j]
            row = pl.multiple_of(slot % 2 * part, part)
            pltpu.make_async_copy(
                arrived_ref.at[slot // 2, pl.ds(row, part)], out_ref.at[j], sem.at[n]
            ).start()
    for n, out_ref in enumerate(refs[:-1]):
        pltpu.make_async_copy(out_ref, out_ref, sem.at[n]).wait()


def first_pass_kernel(scale, count, y_ref, slot_ref, *refs):
    out_ref, total_ref, answer_ref, keys, values, key_sem, sems = refs[-7:]
    latents, first_ref, pieces = refs[:8], refs[8], refs[9 : 9 + count]
    y = y_ref[0]
    blocks, tiles = slot_ref.shape
    rows = keys.shape[2]
    tile_part = rows // PLANES
    piece, block = pl.program_id(0), pl.program_id(1)

    @pl.when((piece == 0) & (block == 0))
    def _():
        for n in range(blocks):
            for turn, ref in enumerate(latents[n * PLANES : (n + 1) * PLANES]):
                row = pl.multiple_of((y + PLANES - turn) % PLANES * tile_part, tile_part)
                pltpu.make_async_copy(ref, keys.at[n, :, pl.ds(row, tile_part)], key_sem.at[n]).start()

            @pl.loop(0, tiles)
            def _(j):
                to = values.at[n, pl.ds(pl.multiple_of(j * rows, rows), rows)]
                pltpu.make_async_copy(first_ref.at[slot_ref[n, j] // 2], to, sems.at[n]).start()

    @pl.when(piece == 0)
    def _():
        pltpu.make_async_copy(keys.at[block], keys.at[block], key_sem.at[block]).wait()
        pltpu.make_async_copy(values.at[block], values.at[block], sems.at[block]).wait()

        @pl.loop(0, tiles)
        def _(j):
            @pl.when(slot_ref[block, j] % 2 == 1)
            def _():
                values[block, pl.ds(pl.multiple_of(j * rows, rows), rows), :] = jnp.zeros(
                    (rows, values.shape[2]), values.dtype
                )

    nt = (((1,), (1,)), ((), ()))
    group = 2
    span = group * rows
    first = pieces[0][...]
    if len(pieces) == 4:
        first = jnp.concatenate([first, pieces[1][...]], axis=0)
    second = jnp.concatenate([pieces[-2][...], pieces[-1][...]], axis=0)
    q = jnp.where(piece == 0, first, second)
    sources, part, width = q.shape
    q = q.reshape(sources * part, width)
    total = jnp.zeros((sources * part, rows), jnp.float32)
    weighted = jnp.zeros((sources * part, values.shape[2]), jnp.float32)
    for at in range(tiles // group):
        k = keys[block, at * group : (at + 1) * group].reshape(span, width)
        s = lax.dot_general(q, k, nt, preferred_element_type=jnp.float32)
        e = jnp.exp2(s * scale)
        for g in range(group):
            counted = (slot_ref[block, at * group + g] % 2 == 0).astype(jnp.float32)
            total = total + e[:, g * rows : (g + 1) * rows] * counted
        weighted = weighted + jnp.dot(
            e.astype(jnp.bfloat16), values[block, at * span : (at + 1) * span], preferred_element_type=jnp.float32
        )
    total = jnp.sum(total, axis=1, keepdims=True)
    out_ref[0] = weighted
    total_ref[0] = jnp.broadcast_to(total, total_ref.shape[1:])
    answer_ref[...] = (weighted * (1.0 / total)).astype(jnp.bfloat16).reshape(answer_ref.shape)


def finish_kernel(scale, turns_ref, y_ref, slot_ref, sum_ref, total_ref, *refs):
    pieces, latents, second_ref = refs[:7], refs[7:15], refs[15]
    out_ref, weighted, total, queries, keys, values, sems, tile_sem = refs[17:]
    y = y_ref[0]
    blocks, tiles = slot_ref.shape
    rows = keys.shape[1]
    tile_part = rows // PLANES
    turn_no, piece = pl.program_id(0), pl.program_id(1)
    block = turns_ref[turn_no]
    live = (turn_no == 0) | (block != turns_ref[0])
    sources, part, width = queries.shape[1:]
    chunk = 256

    @pl.when((piece == 0) & live)
    def _():
        own = pl.ds(pl.multiple_of(block * part, part), part)
        for p in range(PLANES):
            if p == 0:
                pltpu.make_async_copy(pieces[p].at[:, own], queries.at[p], sems.at[p]).start()
            else:
                mid = sources // 2
                for h in range(2):
                    to = queries.at[p, pl.ds(h * mid, mid)]
                    pltpu.make_async_copy(pieces[2 * p - 1 + h].at[:, own], to, sems.at[p]).start()
            for at in range(0, weighted.shape[1], chunk):
                some = pl.ds(at, chunk)
                pltpu.make_async_copy(sum_ref.at[blocks * p + block, some], weighted.at[p, some], sems.at[p]).start()
                pltpu.make_async_copy(total_ref.at[blocks * p + block, some], total.at[p, some], sems.at[p]).start()
            if p > 0:
                continue
            for n in range(blocks):

                @pl.when(block == n)
                def _():
                    @pl.loop(0, tiles)
                    def _(j):
                        slot = slot_ref[n, j]

                        @pl.when(slot % 2 == 1)
                        def _():
                            for turn, ref in enumerate(latents[n * PLANES : (n + 1) * PLANES]):
                                row = pl.multiple_of((y + PLANES - turn) % PLANES * tile_part, tile_part)
                                pltpu.make_async_copy(ref.at[j], keys.at[j, pl.ds(row, tile_part)], tile_sem).start()
                            pltpu.make_async_copy(second_ref.at[slot // 2], values.at[j], tile_sem).start()

        @pl.loop(0, tiles)
        def _(j):
            @pl.when(slot_ref[block, j] % 2 == 1)
            def _():
                pltpu.make_async_copy(keys.at[j], keys.at[j], tile_sem).wait()
                pltpu.make_async_copy(values.at[j], values.at[j], tile_sem).wait()

    @pl.when(live)
    def _():
        for held in (queries, weighted, total):
            pltpu.make_async_copy(held.at[piece], held.at[piece], sems.at[piece]).wait()
        nt = (((1,), (1,)), ((), ()))
        lanes = total.shape[2]

        @pl.loop(0, tiles)
        def _(j):
            @pl.when(slot_ref[block, j] % 2 == 1)
            def _():
                q = queries[piece].reshape(sources * part, width)
                s = lax.dot_general(q, keys[j], nt, preferred_element_type=jnp.float32)
                e = jnp.exp2(s * scale)
                total[piece] += jnp.sum(e, axis=1, keepdims=True)
                weighted[piece] += jnp.dot(e.astype(jnp.bfloat16), values[j], preferred_element_type=jnp.float32)

        share = 1.0 / total[piece]
        for at in range(0, weighted.shape[2], lanes):
            out_ref[:, :, at : at + lanes] = (
                (weighted[piece, :, at : at + lanes] * share).astype(jnp.bfloat16).reshape(sources, part, lanes)
            )


def unpack_kernel(pos_ref, in_ref, out_ref, table, got):
    lanes = 128
    step = 256

    @pl.loop(0, in_ref.shape[0] // step)
    def _(c):
        at = pl.ds(pl.multiple_of(c * step, step), step)
        to = pl.multiple_of(2 * c * step, 2 * step)
        table[pl.ds(to, step, stride=2), :] = in_ref[at, :lanes].astype(jnp.float32)
        table[pl.ds(to + 1, step, stride=2), :] = in_ref[at, lanes:].astype(jnp.float32)

    count = out_ref.shape[0]

    @pl.loop(0, count // 32)
    def _(c):
        at = pl.multiple_of(c * 64, 64)
        for r in range(32):
            i = pl.multiple_of(pos_ref[0, c * 32 + r], 2)
            got[pl.ds(at + 2 * r, 2), :] = table[pl.ds(i, 2), :]

    @pl.loop(0, count // step)
    def _(c):
        at = pl.multiple_of(c * step, step)
        out_ref[pl.ds(at, step), :lanes] = got[pl.ds(2 * at, step, stride=2), :].astype(jnp.bfloat16)
        out_ref[pl.ds(at, step), lanes:] = got[pl.ds(2 * at + 1, step, stride=2), :].astype(jnp.bfloat16)


def shards(queries, cluster, anchor_latent, anchor_labels, tile_list):
    dp_count = lax.axis_size("dp")
    y = lax.axis_index("label").astype(jnp.int32)
    y1 = y.reshape(1)
    query_count, width = queries.shape
    blocks_here, tiles_each = tile_list.shape
    blocks = blocks_here * dp_count
    capacity = 2 * query_count // blocks
    part = capacity // PLANES
    tiles_here = anchor_latent.shape[0] // TILE
    tile_part = TILE // PLANES
    columns = anchor_labels.shape[1]
    wanted_count = blocks_here * tiles_each
    slots = 2

    wanted = tile_list.reshape(wanted_count)
    source = wanted // tiles_here
    number = jnp.arange(wanted_count, dtype=jnp.int32)
    order = jnp.sum(
        ((source[:, None] == source[None, :]) & (number[None, :] < number[:, None])).astype(jnp.int32), axis=1
    )
    slot_of = source * slots + order
    slot_table = slot_of.reshape(blocks_here, tiles_each)

    own = blocks_here * part
    sent, pos = pl.pallas_call(
        functools.partial(pack_kernel, blocks, part, tiles_here),
        in_specs=[SMEM, VMEM, VMEM, ANY],
        out_specs=[VMEM, VMEM],
        out_shape=[
            jax.ShapeDtypeStruct((dp_count, own + 8, width), jnp.bfloat16),
            jax.ShapeDtypeStruct((1, query_count), jnp.int32),
        ],
        scratch_shapes=[
            pltpu.VMEM((query_count, width), jnp.bfloat16),
            pltpu.VMEM((2 * query_count, 128), jnp.float32),
            pltpu.VMEM((2 * blocks * part, 128), jnp.float32),
            pltpu.VMEM((blocks, 128), jnp.int32),
            pltpu.SMEM((blocks, 128), jnp.int32),
            pltpu.SemaphoreType.DMA,
            pltpu.SemaphoreType.DMA,
        ],
        compiler_params=params(FULL),
        name="pack",
    )(y1, cluster.reshape(1, query_count), tile_list, queries)
    arrived = lax.all_to_all(sent, "dp", split_axis=0, concat_axis=0, tiled=True)
    asked = arrived[:, own, :: width // slots].astype(jnp.int32)

    quarter = lax.dynamic_slice_in_dim(anchor_latent.reshape(tiles_here, TILE, width), y * tile_part, tile_part, axis=1)
    label_tiles = anchor_labels.reshape(tiles_here, TILE, columns)

    def exchange(v):
        return lax.all_to_all(v, "dp", split_axis=0, concat_axis=0, tiled=True)

    def tiles_out(kernel, tiles, rows):
        return pl.pallas_call(
            kernel,
            in_specs=[SMEM, VMEM],
            out_specs=ANY,
            out_shape=jax.ShapeDtypeStruct((dp_count, rows, tiles.shape[2]), jnp.bfloat16),
            scratch_shapes=[pltpu.SemaphoreType.DMA],
            compiler_params=params(8),
        )(asked, tiles)

    got_latents = exchange(tiles_out(slots_kernel, unit_rows(quarter), slots * tile_part))
    first_out = tiles_out(functools.partial(one_slot_kernel, 0), label_tiles, TILE)
    second_out = tiles_out(functools.partial(one_slot_kernel, 1), label_tiles, TILE)

    def shift(v, by):
        return lax.ppermute(v, "label", [(i, (i + by) % PLANES) for i in range(PLANES)])

    mid = dp_count // 2
    q0a, q0b = arrived[:mid, :own], arrived[mid:, :own]
    q1a, q3b, q1b, q3a = shift(q0a, 1), shift(q0b, 3), shift(q0b, 1), shift(q0a, 3)
    got_first = exchange(first_out)
    k0 = pl.pallas_call(
        pick_kernel,
        in_specs=[SMEM, ANY],
        out_specs=[VMEM] * blocks_here,
        out_shape=[jax.ShapeDtypeStruct((tiles_each, tile_part, width), jnp.bfloat16)] * blocks_here,
        scratch_shapes=[pltpu.SemaphoreType.DMA((blocks_here,))],
        compiler_params=params(FULL),
        name="pick",
    )(slot_table, got_latents)
    k1a, k3b = shift(k0[0], 1), shift(k0[1], 3)
    k1b, k3a = shift(k0[1], 1), shift(k0[0], 3)
    k2a, k2b = shift(k1a, 1), shift(k3b, 3)
    got_second = exchange(second_out)
    latents = [k0[0], k1a, k2a, k3a, k0[1], k1b, k2b, k3b]
    q2a, q2b = shift(q1a, 1), shift(q3b, 3)

    rows = dp_count * part
    keys = tiles_each * TILE
    scale = LOG2E / (width * kernel_width)

    def first_pass(begin, pieces, sums):
        piece = pl.BlockSpec((dp_count, part, width), lambda p, n: (0, n, 0))
        half = pl.BlockSpec((mid, part, width), lambda p, n: (0, n, 0))
        specs = [piece, half, half] if len(pieces) == 3 else [half] * 4
        given = 2 + 9 + len(pieces)
        return pl.pallas_call(
            functools.partial(first_pass_kernel, scale, len(pieces)),
            grid=(2, blocks_here),
            in_specs=[SMEM, SMEM] + [ANY] * 9 + specs + [ANY] * len(sums),
            out_specs=[
                pl.BlockSpec((1, rows, columns), lambda p, n: (blocks_here * (begin + p) + n, 0, 0)),
                pl.BlockSpec((1, rows, 128), lambda p, n: (blocks_here * (begin + p) + n, 0, 0)),
                pl.BlockSpec((dp_count, part, columns), lambda p, n: (0, blocks_here * (begin + p) + n, 0)),
            ],
            out_shape=[
                jax.ShapeDtypeStruct((PLANES * blocks_here, rows, columns), jnp.float32),
                jax.ShapeDtypeStruct((PLANES * blocks_here, rows, 128), jnp.float32),
                jax.ShapeDtypeStruct((dp_count, PLANES * own, columns), jnp.bfloat16),
            ],
            scratch_shapes=[
                pltpu.VMEM((blocks_here, tiles_each, TILE, width), jnp.bfloat16),
                pltpu.VMEM((blocks_here, keys, columns), jnp.bfloat16),
                pltpu.SemaphoreType.DMA((blocks_here,)),
                pltpu.SemaphoreType.DMA((blocks_here,)),
            ],
            input_output_aliases={given + i: i for i in range(len(sums))},
            compiler_params=params(FULL),
            cost_estimate=pl.CostEstimate(
                flops=4 * blocks_here * rows * keys * (width + columns),
                transcendentals=2 * blocks_here * rows * keys,
                bytes_accessed=2 * blocks_here * keys * (width + columns),
            ),
            name="first_pass",
        )(y1, slot_table, *latents, got_first, *pieces, *sums)

    sums = first_pass(0, (arrived, q1a, q1b), ())
    *sums, answers = first_pass(2, (q3a, q3b, q2a, q2b), sums)

    has = jnp.sum(slot_table % 2, axis=1) > 0
    lead = jnp.where(has[0], 0, jnp.where(has[1], 1, 0))
    turns = jnp.stack([lead, jnp.where(has[0] & has[1], 1, lead)]).astype(jnp.int32)

    def answer_block(n, p, t):
        repeated = (n > 0) & (t[n] == t[0])
        return (0, jnp.where(repeated, blocks_here * (PLANES - 1) + t[0], blocks_here * p + t[n]), 0)

    answers = pl.pallas_call(
        functools.partial(finish_kernel, scale),
        grid_spec=pltpu.PrefetchScalarGridSpec(
            num_scalar_prefetch=1,
            grid=(blocks_here, PLANES),
            in_specs=[SMEM, SMEM] + [ANY] * 19,
            out_specs=pl.BlockSpec((dp_count, part, columns), answer_block),
            scratch_shapes=[
                pltpu.VMEM((PLANES, rows, columns), jnp.float32),
                pltpu.VMEM((PLANES, rows, 128), jnp.float32),
                pltpu.VMEM((PLANES, dp_count, part, width), jnp.bfloat16),
                pltpu.VMEM((tiles_each, TILE, width), jnp.bfloat16),
                pltpu.VMEM((tiles_each, TILE, columns), jnp.bfloat16),
                pltpu.SemaphoreType.DMA((PLANES,)),
                pltpu.SemaphoreType.DMA,
            ],
        ),
        out_shape=jax.ShapeDtypeStruct((dp_count, PLANES * own, columns), jnp.bfloat16),
        input_output_aliases={5 + 7 + 9: 0},
        compiler_params=params(FULL),
        name="finish",
    )(turns, y1, slot_table, *sums, arrived, q1a, q1b, q3a, q3b, q2a, q2b, *latents, got_second, answers)
    back = exchange(answers)
    count = back.shape[0] * back.shape[1]
    return pl.pallas_call(
        unpack_kernel,
        in_specs=[SMEM, VMEM],
        out_specs=VMEM,
        out_shape=jax.ShapeDtypeStruct((query_count, columns), jnp.bfloat16),
        scratch_shapes=[
            pltpu.VMEM((2 * count, 128), jnp.float32),
            pltpu.VMEM((2 * query_count, 128), jnp.float32),
        ],
        compiler_params=params(24),
        name="unpack",
    )(pos, back.reshape(count, columns))


def solution(mesh):
    placed = (P("dp", None), P("dp", None), P("dp", None), P("dp", "label"), P("dp", None))
    return jax.shard_map(shards, mesh=mesh, in_specs=placed, out_specs=P("dp", "label"), check_vma=False)
```

```python
import functools
import jax
import jax.numpy as jnp
from jax import lax
from jax.sharding import PartitionSpec as P
from jax.experimental import pallas as pl
from jax.experimental.pallas import tpu as pltpu

TILE = 128
kernel_width = 0.025
norm_epsilon = 1e-05
PLANES = 4
FULL = 64
LOG2E = 1.4426950408889634
VMEM = pl.BlockSpec(memory_space=pltpu.VMEM)
ANY = pl.BlockSpec(memory_space=pl.ANY)
SMEM = pl.BlockSpec(memory_space=pltpu.SMEM)


def unit_rows(values):
    widened = values.astype(jnp.float32)
    scaled = widened * lax.rsqrt(jnp.mean(widened * widened, axis=-1, keepdims=True) + norm_epsilon)
    return scaled.astype(jnp.bfloat16)


def params(mib, **kw):
    return pltpu.CompilerParams(vmem_limit_bytes=min(mib * 1024 * 1024, 67043328), **kw)


def pack_kernel(
    blocks, part, tiles_here, y_ref, ids_ref, list_ref, x_ref,
    out_ref, pos_ref, rows, table, got, hold, inv, row_sem, inv_sem,
):
    load = pltpu.make_async_copy(x_ref, rows, row_sem)
    load.start()
    y = y_ref[0]
    lanes = 128
    own = 2 * part
    wanted = list_ref[...]
    wanted = jnp.concatenate([wanted[n : n + 1] for n in range(wanted.shape[0])], axis=1)
    many = wanted.shape[1]
    across = lax.broadcasted_iota(jnp.int32, (many, many), 1)
    down = lax.broadcasted_iota(jnp.int32, (many, many), 0)
    source = wanted // tiles_here
    upright = jnp.sum(jnp.where(across == down, source.astype(jnp.float32), 0.0), axis=1, keepdims=True)
    same = (upright.astype(jnp.int32) == source) & (down < across)
    order = jnp.sum(same.astype(jnp.float32), axis=0, keepdims=True)
    holders, told_rows = out_ref.shape[0], out_ref.shape[1] - own
    holder = lax.broadcasted_iota(jnp.int32, (holders, many), 0) == source
    number = (wanted % tiles_here).astype(jnp.float32)
    for k in range(2):
        told = jnp.sum(jnp.where(holder & (order == k), number, 0.0), axis=1, keepdims=True)
        told = jnp.broadcast_to(told[:, :, None], (holders, told_rows, lanes))
        out_ref[:, own:, k * lanes : (k + 1) * lanes] = told.astype(jnp.bfloat16)

    count = ids_ref.shape[1]
    step = 256
    upper = (
        lax.broadcasted_iota(jnp.int32, (step, step), 0)
        <= lax.broadcasted_iota(jnp.int32, (step, step), 1)
    ).astype(jnp.bfloat16)
    block_no = lax.broadcasted_iota(jnp.int32, (blocks, step), 0)
    slot_no = lax.broadcasted_iota(jnp.int32, (lanes, step), 0) + part * y
    lane = lax.broadcasted_iota(jnp.int32, (1, step), 1)
    carry = jnp.zeros((blocks, 1), jnp.float32)
    high = jnp.zeros((blocks, lanes), jnp.float32)
    low = jnp.zeros((blocks, lanes), jnp.float32)
    nt = (((1,), (1,)), ((), ()))
    for c in range(count // step):
        ids = ids_ref[:, c * step : (c + 1) * step]
        hit = block_no == ids
        hits = hit.astype(jnp.bfloat16)
        upto = jnp.dot(hits, upper, preferred_element_type=jnp.float32)
        rank = jnp.sum(jnp.where(hit, upto + carry, 0.0), axis=0, keepdims=True)
        rank = rank.astype(jnp.int32) - 1
        carry = carry + upto[:, step - 1 : step]
        turn = (y + PLANES - rank // part) % PLANES
        place = jnp.where(turn < 2, turn, 5 - turn)
        pos_ref[:, c * step : (c + 1) * step] = 2 * (
            ids // 2 * (2 * PLANES * part)
            + place * (2 * part)
            + ids % 2 * part
            + rank % part
        )
        row = lane + c * step
        chosen = (slot_no == rank).astype(jnp.bfloat16)
        row_high = (row // 64).astype(jnp.float32)
        row_low = (row % 64).astype(jnp.float32)
        high += lax.dot_general(
            jnp.where(hit, row_high, 0.0).astype(jnp.bfloat16), chosen, nt, preferred_element_type=jnp.float32
        )
        low += lax.dot_general(
            jnp.where(hit, row_low, 0.0).astype(jnp.bfloat16), chosen, nt, preferred_element_type=jnp.float32
        )
    hold[...] = high.astype(jnp.int32) * 128 + low.astype(jnp.int32) * 2
    tell = pltpu.make_async_copy(hold, inv, inv_sem)
    tell.start()
    load.wait()

    @pl.loop(0, count // step)
    def _(c):
        at = pl.ds(pl.multiple_of(c * step, step), step)
        to = pl.multiple_of(2 * c * step, 2 * step)
        table[pl.ds(to, step, stride=2), :] = rows[at, :lanes].astype(jnp.float32)
        table[pl.ds(to + 1, step, stride=2), :] = rows[at, lanes:].astype(jnp.float32)

    tell.wait()

    @pl.loop(0, blocks)
    def _(b):
        at = pl.multiple_of(2 * b * part, 2 * part)
        for r in range(part):
            i = pl.multiple_of(inv[b, r], 2)
            got[pl.ds(at + 2 * r, 2), :] = table[pl.ds(i, 2), :]

    width = 2 * lanes
    some = 4

    @pl.loop(0, out_ref.shape[0] // some)
    def _(g):
        at = pl.multiple_of(2 * g * some * own, 2 * some * own)
        a = got[pl.ds(at, some * own, stride=2), :]
        b = got[pl.ds(at + 1, some * own, stride=2), :]
        scale = lax.rsqrt(jnp.sum(a * a + b * b, axis=-1, keepdims=True) / width + norm_epsilon)
        to = pl.ds(g * some, some)
        out_ref[to, :own, :lanes] = (a * scale).astype(jnp.bfloat16).reshape(some, own, lanes)
        out_ref[to, :own, lanes:] = (b * scale).astype(jnp.bfloat16).reshape(some, own, lanes)


def slots_kernel(asked_ref, tile_ref, out_ref, sem):
    dests, slots = asked_ref.shape
    part = tile_ref.shape[1]
    for d in range(dests):
        for s in range(slots):
            pltpu.make_async_copy(tile_ref.at[asked_ref[d, s]], out_ref.at[d, pl.ds(s * part, part)], sem).start()
    pltpu.make_async_copy(out_ref, out_ref, sem).wait()


def one_slot_kernel(slot, asked_ref, tile_ref, out_ref, sem):
    for d in range(asked_ref.shape[0]):
        pltpu.make_async_copy(tile_ref.at[asked_ref[d, slot]], out_ref.at[d], sem).start()
    pltpu.make_async_copy(out_ref, out_ref, sem).wait()


def pick_kernel(slot_ref, arrived_ref, *refs):
    blocks, tiles = slot_ref.shape
    turns_ref, sem = refs[-2:]
    part = refs[0].shape[1]
    for n, out_ref in enumerate(refs[:-2]):
        for j in range(tiles):
            slot = slot_ref[n, j]
            row = pl.multiple_of(slot % 2 * part, part)
            pltpu.make_async_copy(
                arrived_ref.at[slot // 2, pl.ds(row, part)], out_ref.at[j], sem.at[n]
            ).start()
    one, two = (sum(slot_ref[n, j] % 2 for j in range(tiles)) for n in range(blocks))
    lead = jnp.where((one == 0) & (two > 0), 1, 0)
    turns_ref[0] = lead
    turns_ref[1] = jnp.where((one > 0) & (two > 0), 1, lead)
    for n, out_ref in enumerate(refs[:-2]):
        pltpu.make_async_copy(out_ref, out_ref, sem.at[n]).wait()


def first_pass_kernel(scale, y_ref, slot_ref, *refs):
    out_ref, total_ref, answer_ref, keys, values, key_sem, sems = refs[-7:]
    latents, first_ref, pieces = refs[:8], refs[8], refs[9:16]
    y = y_ref[0]
    blocks, tiles = slot_ref.shape
    rows = keys.shape[2]
    tile_part = rows // PLANES
    piece, block = pl.program_id(0), pl.program_id(1)

    @pl.when((piece == 0) & (block == 0))
    def _():
        for n in range(blocks):
            for turn, ref in enumerate(latents[n * PLANES : (n + 1) * PLANES]):
                row = pl.multiple_of((y + PLANES - turn) % PLANES * tile_part, tile_part)
                pltpu.make_async_copy(ref, keys.at[n, :, pl.ds(row, tile_part)], key_sem.at[n]).start()

            @pl.loop(0, tiles)
            def _(j):
                to = values.at[n, pl.ds(pl.multiple_of(j * rows, rows), rows)]
                pltpu.make_async_copy(first_ref.at[slot_ref[n, j] // 2], to, sems.at[n]).start()

    @pl.when(piece == 0)
    def _():
        pltpu.make_async_copy(keys.at[block], keys.at[block], key_sem.at[block]).wait()
        pltpu.make_async_copy(values.at[block], values.at[block], sems.at[block]).wait()

        @pl.loop(0, tiles)
        def _(j):
            @pl.when(slot_ref[block, j] % 2 == 1)
            def _():
                values[block, pl.ds(pl.multiple_of(j * rows, rows), rows), :] = jnp.zeros(
                    (rows, values.shape[2]), values.dtype
                )

    nt = (((1,), (1,)), ((), ()))
    group = 2
    span = group * rows
    q = pieces[0][...]
    for p in range(1, PLANES):
        other = jnp.concatenate([pieces[2 * p - 1][...], pieces[2 * p][...]], axis=0)
        q = jnp.where(piece == p, other, q)
    sources, part, width = q.shape
    q = q.reshape(sources * part, width)
    total = jnp.zeros((sources * part, rows), jnp.float32)
    weighted = jnp.zeros((sources * part, values.shape[2]), jnp.float32)
    for at in range(tiles // group):
        k = keys[block, at * group : (at + 1) * group].reshape(span, width)
        s = lax.dot_general(q, k, nt, preferred_element_type=jnp.float32)
        e = jnp.exp2(s * scale)
        for g in range(group):
            counted = (slot_ref[block, at * group + g] % 2 == 0).astype(jnp.float32)
            total = total + e[:, g * rows : (g + 1) * rows] * counted
        weighted = weighted + jnp.dot(
            e.astype(jnp.bfloat16), values[block, at * span : (at + 1) * span], preferred_element_type=jnp.float32
        )
    total = jnp.sum(total, axis=1, keepdims=True)
    out_ref[0] = weighted
    total_ref[0] = jnp.broadcast_to(total, total_ref.shape[1:])
    answer_ref[...] = (weighted * (1.0 / total)).astype(jnp.bfloat16).reshape(answer_ref.shape)


def finish_kernel(scale, turns_ref, y_ref, slot_ref, sum_ref, total_ref, *refs):
    pieces, latents, second_ref = refs[:7], refs[7:15], refs[15]
    out_ref, weighted, total, queries, keys, values, sems, tile_sem = refs[17:]
    y = y_ref[0]
    blocks, tiles = slot_ref.shape
    rows = keys.shape[1]
    tile_part = rows // PLANES
    turn_no, piece = pl.program_id(0), pl.program_id(1)
    block = turns_ref[turn_no]
    live = (turn_no == 0) | (block != turns_ref[0])
    sources, part, width = queries.shape[1:]
    chunk = 256

    @pl.when((piece == 0) & live)
    def _():
        own = pl.ds(pl.multiple_of(block * part, part), part)
        for p in range(PLANES):
            if p == 0:
                pltpu.make_async_copy(pieces[p].at[:, own], queries.at[p], sems.at[p]).start()
            else:
                mid = sources // 2
                for h in range(2):
                    to = queries.at[p, pl.ds(h * mid, mid)]
                    pltpu.make_async_copy(pieces[2 * p - 1 + h].at[:, own], to, sems.at[p]).start()
            for at in range(0, weighted.shape[1], chunk):
                some = pl.ds(at, chunk)
                pltpu.make_async_copy(sum_ref.at[blocks * p + block, some], weighted.at[p, some], sems.at[p]).start()
                pltpu.make_async_copy(total_ref.at[blocks * p + block, some], total.at[p, some], sems.at[p]).start()
            if p > 0:
                continue
            for n in range(blocks):

                @pl.when(block == n)
                def _():
                    @pl.loop(0, tiles)
                    def _(j):
                        slot = slot_ref[n, j]

                        @pl.when(slot % 2 == 1)
                        def _():
                            for turn, ref in enumerate(latents[n * PLANES : (n + 1) * PLANES]):
                                row = pl.multiple_of((y + PLANES - turn) % PLANES * tile_part, tile_part)
                                pltpu.make_async_copy(ref.at[j], keys.at[j, pl.ds(row, tile_part)], tile_sem).start()
                            pltpu.make_async_copy(second_ref.at[slot // 2], values.at[j], tile_sem).start()

        @pl.loop(0, tiles)
        def _(j):
            @pl.when(slot_ref[block, j] % 2 == 1)
            def _():
                pltpu.make_async_copy(keys.at[j], keys.at[j], tile_sem).wait()
                pltpu.make_async_copy(values.at[j], values.at[j], tile_sem).wait()

    @pl.when(live)
    def _():
        for held in (queries, weighted, total):
            pltpu.make_async_copy(held.at[piece], held.at[piece], sems.at[piece]).wait()
        nt = (((1,), (1,)), ((), ()))
        lanes = total.shape[2]

        @pl.loop(0, tiles)
        def _(j):
            @pl.when(slot_ref[block, j] % 2 == 1)
            def _():
                q = queries[piece].reshape(sources * part, width)
                s = lax.dot_general(q, keys[j], nt, preferred_element_type=jnp.float32)
                e = jnp.exp2(s * scale)
                total[piece] += jnp.sum(e, axis=1, keepdims=True)
                weighted[piece] += jnp.dot(e.astype(jnp.bfloat16), values[j], preferred_element_type=jnp.float32)

        share = 1.0 / total[piece]
        for at in range(0, weighted.shape[2], lanes):
            out_ref[:, :, at : at + lanes] = (
                (weighted[piece, :, at : at + lanes] * share).astype(jnp.bfloat16).reshape(sources, part, lanes)
            )


def unpack_kernel(pos_ref, in_ref, out_ref, table, got):
    lanes = 128
    step = 256

    @pl.loop(0, in_ref.shape[0] // step)
    def _(c):
        at = pl.ds(pl.multiple_of(c * step, step), step)
        to = pl.multiple_of(2 * c * step, 2 * step)
        table[pl.ds(to, step, stride=2), :] = in_ref[at, :lanes].astype(jnp.float32)
        table[pl.ds(to + 1, step, stride=2), :] = in_ref[at, lanes:].astype(jnp.float32)

    count = out_ref.shape[0]

    @pl.loop(0, count // 32)
    def _(c):
        at = pl.multiple_of(c * 64, 64)
        for r in range(32):
            i = pl.multiple_of(pos_ref[0, c * 32 + r], 2)
            got[pl.ds(at + 2 * r, 2), :] = table[pl.ds(i, 2), :]

    @pl.loop(0, count // step)
    def _(c):
        at = pl.multiple_of(c * step, step)
        out_ref[pl.ds(at, step), :lanes] = got[pl.ds(2 * at, step, stride=2), :].astype(jnp.bfloat16)
        out_ref[pl.ds(at, step), lanes:] = got[pl.ds(2 * at + 1, step, stride=2), :].astype(jnp.bfloat16)


def shards(queries, cluster, anchor_latent, anchor_labels, tile_list):
    dp_count = lax.axis_size("dp")
    y = lax.axis_index("label").astype(jnp.int32)
    y1 = y.reshape(1)
    query_count, width = queries.shape
    blocks_here, tiles_each = tile_list.shape
    blocks = blocks_here * dp_count
    capacity = 2 * query_count // blocks
    part = capacity // PLANES
    tiles_here = anchor_latent.shape[0] // TILE
    tile_part = TILE // PLANES
    columns = anchor_labels.shape[1]
    wanted_count = blocks_here * tiles_each
    slots = 2

    wanted = tile_list.reshape(wanted_count)
    source = wanted // tiles_here
    number = jnp.arange(wanted_count, dtype=jnp.int32)
    order = jnp.sum(
        ((source[:, None] == source[None, :]) & (number[None, :] < number[:, None])).astype(jnp.int32), axis=1
    )
    slot_of = source * slots + order
    slot_table = slot_of.reshape(blocks_here, tiles_each)

    own = blocks_here * part
    sent, pos = pl.pallas_call(
        functools.partial(pack_kernel, blocks, part, tiles_here),
        in_specs=[SMEM, VMEM, VMEM, ANY],
        out_specs=[VMEM, VMEM],
        out_shape=[
            jax.ShapeDtypeStruct((dp_count, own + 8, width), jnp.bfloat16),
            jax.ShapeDtypeStruct((1, query_count), jnp.int32),
        ],
        scratch_shapes=[
            pltpu.VMEM((query_count, width), jnp.bfloat16),
            pltpu.VMEM((2 * query_count, 128), jnp.float32),
            pltpu.VMEM((2 * blocks * part, 128), jnp.float32),
            pltpu.VMEM((blocks, 128), jnp.int32),
            pltpu.SMEM((blocks, 128), jnp.int32),
            pltpu.SemaphoreType.DMA,
            pltpu.SemaphoreType.DMA,
        ],
        compiler_params=params(FULL),
        name="pack",
    )(y1, cluster.reshape(1, query_count), tile_list, queries)
    arrived = lax.all_to_all(sent, "dp", split_axis=0, concat_axis=0, tiled=True)
    asked = arrived[:, own, :: width // slots].astype(jnp.int32)

    quarter = lax.dynamic_slice_in_dim(anchor_latent.reshape(tiles_here, TILE, width), y * tile_part, tile_part, axis=1)
    label_tiles = anchor_labels.reshape(tiles_here, TILE, columns)

    def exchange(v):
        return lax.all_to_all(v, "dp", split_axis=0, concat_axis=0, tiled=True)

    def tiles_out(kernel, tiles, rows):
        return pl.pallas_call(
            kernel,
            in_specs=[SMEM, VMEM],
            out_specs=ANY,
            out_shape=jax.ShapeDtypeStruct((dp_count, rows, tiles.shape[2]), jnp.bfloat16),
            scratch_shapes=[pltpu.SemaphoreType.DMA],
            compiler_params=params(8),
        )(asked, tiles)

    got_latents = exchange(tiles_out(slots_kernel, unit_rows(quarter), slots * tile_part))
    first_out = tiles_out(functools.partial(one_slot_kernel, 0), label_tiles, TILE)
    second_out = tiles_out(functools.partial(one_slot_kernel, 1), label_tiles, TILE)

    def shift(v, by):
        return lax.ppermute(v, "label", [(i, (i + by) % PLANES) for i in range(PLANES)])

    mid = dp_count // 2
    q0a, q0b = arrived[:mid, :own], arrived[mid:, :own]
    q1a, q3b, q1b, q3a = shift(q0a, 1), shift(q0b, 3), shift(q0b, 1), shift(q0a, 3)
    got_first = exchange(first_out)
    *k0, turns = pl.pallas_call(
        pick_kernel,
        in_specs=[SMEM, ANY],
        out_specs=[VMEM] * blocks_here + [SMEM],
        out_shape=[jax.ShapeDtypeStruct((tiles_each, tile_part, width), jnp.bfloat16)] * blocks_here
        + [jax.ShapeDtypeStruct((blocks_here,), jnp.int32)],
        scratch_shapes=[pltpu.SemaphoreType.DMA((blocks_here,))],
        compiler_params=params(FULL),
        name="pick",
    )(slot_table, got_latents)
    k1a, k3b = shift(k0[0], 1), shift(k0[1], 3)
    k1b, k3a = shift(k0[1], 1), shift(k0[0], 3)
    k2a, k2b = shift(k1a, 1), shift(k3b, 3)
    got_second = exchange(second_out)
    latents = [k0[0], k1a, k2a, k3a, k0[1], k1b, k2b, k3b]
    q2a, q2b = shift(q1a, 1), shift(q3b, 3)

    rows = dp_count * part
    keys = tiles_each * TILE
    scale = LOG2E / (width * kernel_width)

    def rows_of(piece, sources):
        return pl.BlockSpec(
            (sources, part, width),
            lambda p, n: (0, jnp.where(p == piece, n, jnp.where(p < piece, 0, blocks_here - 1)), 0),
        )

    pieces = [arrived, q1a, q1b, q3a, q3b, q2a, q2b]
    *sums, answers = pl.pallas_call(
        functools.partial(first_pass_kernel, scale),
        grid=(PLANES, blocks_here),
        in_specs=[SMEM, SMEM]
        + [ANY] * 9
        + [rows_of(0, dp_count)]
        + [rows_of(p, mid) for p in range(1, PLANES) for _ in range(2)],
        out_specs=[
            pl.BlockSpec((1, rows, columns), lambda p, n: (blocks_here * p + n, 0, 0)),
            pl.BlockSpec((1, rows, 128), lambda p, n: (blocks_here * p + n, 0, 0)),
            pl.BlockSpec((dp_count, part, columns), lambda p, n: (0, blocks_here * p + n, 0)),
        ],
        out_shape=[
            jax.ShapeDtypeStruct((PLANES * blocks_here, rows, columns), jnp.float32),
            jax.ShapeDtypeStruct((PLANES * blocks_here, rows, 128), jnp.float32),
            jax.ShapeDtypeStruct((dp_count, PLANES * own, columns), jnp.bfloat16),
        ],
        scratch_shapes=[
            pltpu.VMEM((blocks_here, tiles_each, TILE, width), jnp.bfloat16),
            pltpu.VMEM((blocks_here, keys, columns), jnp.bfloat16),
            pltpu.SemaphoreType.DMA((blocks_here,)),
            pltpu.SemaphoreType.DMA((blocks_here,)),
        ],
        compiler_params=params(FULL),
        cost_estimate=pl.CostEstimate(
            flops=2 * PLANES * blocks_here * rows * keys * (width + columns),
            transcendentals=PLANES * blocks_here * rows * keys,
            bytes_accessed=6 * PLANES * blocks_here * rows * columns,
        ),
        name="first_pass",
    )(y1, slot_table, *latents, got_first, *pieces)

    def answer_block(n, p, t):
        repeated = (n > 0) & (t[n] == t[0])
        return (0, jnp.where(repeated, blocks_here * (PLANES - 1) + t[0], blocks_here * p + t[n]), 0)

    answers = pl.pallas_call(
        functools.partial(finish_kernel, scale),
        grid_spec=pltpu.PrefetchScalarGridSpec(
            num_scalar_prefetch=1,
            grid=(blocks_here, PLANES),
            in_specs=[SMEM, SMEM] + [ANY] * 19,
            out_specs=pl.BlockSpec((dp_count, part, columns), answer_block),
            scratch_shapes=[
                pltpu.VMEM((PLANES, rows, columns), jnp.float32),
                pltpu.VMEM((PLANES, rows, 128), jnp.float32),
                pltpu.VMEM((PLANES, dp_count, part, width), jnp.bfloat16),
                pltpu.VMEM((tiles_each, TILE, width), jnp.bfloat16),
                pltpu.VMEM((tiles_each, TILE, columns), jnp.bfloat16),
                pltpu.SemaphoreType.DMA((PLANES,)),
                pltpu.SemaphoreType.DMA,
            ],
        ),
        out_shape=jax.ShapeDtypeStruct((dp_count, PLANES * own, columns), jnp.bfloat16),
        input_output_aliases={5 + 7 + 9: 0},
        compiler_params=params(FULL),
        name="finish",
    )(turns, y1, slot_table, *sums, *pieces, *latents, got_second, answers)
    back = exchange(answers)
    count = back.shape[0] * back.shape[1]
    return pl.pallas_call(
        unpack_kernel,
        in_specs=[SMEM, VMEM],
        out_specs=VMEM,
        out_shape=jax.ShapeDtypeStruct((query_count, columns), jnp.bfloat16),
        scratch_shapes=[
            pltpu.VMEM((2 * count, 128), jnp.float32),
            pltpu.VMEM((2 * query_count, 128), jnp.float32),
        ],
        compiler_params=params(24),
        name="unpack",
    )(pos, back.reshape(count, columns))


def solution(mesh):
    placed = (P("dp", None), P("dp", None), P("dp", None), P("dp", "label"), P("dp", None))
    return jax.shard_map(shards, mesh=mesh, in_specs=placed, out_specs=P("dp", "label"), check_vma=False)
```

```python
import functools
import jax
import jax.numpy as jnp
from jax import lax
from jax.sharding import PartitionSpec as P
from jax.experimental import pallas as pl
from jax.experimental.pallas import tpu as pltpu

TILE = 128
kernel_width = 0.025
norm_epsilon = 1e-05
PLANES = 4
FULL = 64
LOG2E = 1.4426950408889634
VMEM = pl.BlockSpec(memory_space=pltpu.VMEM)
ANY = pl.BlockSpec(memory_space=pl.ANY)
SMEM = pl.BlockSpec(memory_space=pltpu.SMEM)


def unit_rows(values):
    widened = values.astype(jnp.float32)
    scaled = widened * lax.rsqrt(jnp.mean(widened * widened, axis=-1, keepdims=True) + norm_epsilon)
    return scaled.astype(jnp.bfloat16)


def params(mib, **kw):
    return pltpu.CompilerParams(vmem_limit_bytes=min(mib * 1024 * 1024, 67043328), **kw)


def pack_kernel(
    blocks, part, tiles_here, y_ref, ids_ref, list_ref, x_ref,
    out_ref, pos_ref, rows, table, got, hold, inv, row_sem, inv_sem,
):
    load = pltpu.make_async_copy(x_ref, rows, row_sem)
    load.start()
    y = y_ref[0]
    lanes = 128
    own = 2 * part
    wanted = list_ref[...]
    wanted = jnp.concatenate([wanted[n : n + 1] for n in range(wanted.shape[0])], axis=1)
    many = wanted.shape[1]
    across = lax.broadcasted_iota(jnp.int32, (many, many), 1)
    down = lax.broadcasted_iota(jnp.int32, (many, many), 0)
    source = wanted // tiles_here
    upright = jnp.sum(jnp.where(across == down, source.astype(jnp.float32), 0.0), axis=1, keepdims=True)
    same = (upright.astype(jnp.int32) == source) & (down < across)
    order = jnp.sum(same.astype(jnp.float32), axis=0, keepdims=True)
    holders, told_rows = out_ref.shape[0], out_ref.shape[1] - own
    holder = lax.broadcasted_iota(jnp.int32, (holders, many), 0) == source
    number = (wanted % tiles_here).astype(jnp.float32)
    for k in range(2):
        told = jnp.sum(jnp.where(holder & (order == k), number, 0.0), axis=1, keepdims=True)
        told = jnp.broadcast_to(told[:, :, None], (holders, told_rows, lanes))
        out_ref[:, own:, k * lanes : (k + 1) * lanes] = told.astype(jnp.bfloat16)

    count = ids_ref.shape[1]
    step = 256
    upper = (
        lax.broadcasted_iota(jnp.int32, (step, step), 0)
        <= lax.broadcasted_iota(jnp.int32, (step, step), 1)
    ).astype(jnp.bfloat16)
    block_no = lax.broadcasted_iota(jnp.int32, (blocks, step), 0)
    slot_no = lax.broadcasted_iota(jnp.int32, (lanes, step), 0) + part * y
    lane = lax.broadcasted_iota(jnp.int32, (1, step), 1)
    carry = jnp.zeros((blocks, 1), jnp.float32)
    high = jnp.zeros((blocks, lanes), jnp.float32)
    low = jnp.zeros((blocks, lanes), jnp.float32)
    nt = (((1,), (1,)), ((), ()))
    for c in range(count // step):
        ids = ids_ref[:, c * step : (c + 1) * step]
        hit = block_no == ids
        hits = hit.astype(jnp.bfloat16)
        upto = jnp.dot(hits, upper, preferred_element_type=jnp.float32)
        rank = jnp.sum(jnp.where(hit, upto + carry, 0.0), axis=0, keepdims=True)
        rank = rank.astype(jnp.int32) - 1
        carry = carry + upto[:, step - 1 : step]
        turn = (y + PLANES - rank // part) % PLANES
        place = jnp.where(turn < 2, turn, 5 - turn)
        pos_ref[:, c * step : (c + 1) * step] = 2 * (
            ids // 2 * (2 * PLANES * part)
            + place * (2 * part)
            + ids % 2 * part
            + rank % part
        )
        row = lane + c * step
        chosen = (slot_no == rank).astype(jnp.bfloat16)
        row_high = (row // 64).astype(jnp.float32)
        row_low = (row % 64).astype(jnp.float32)
        high += lax.dot_general(
            jnp.where(hit, row_high, 0.0).astype(jnp.bfloat16), chosen, nt, preferred_element_type=jnp.float32
        )
        low += lax.dot_general(
            jnp.where(hit, row_low, 0.0).astype(jnp.bfloat16), chosen, nt, preferred_element_type=jnp.float32
        )
    hold[...] = high.astype(jnp.int32) * 128 + low.astype(jnp.int32) * 2
    tell = pltpu.make_async_copy(hold, inv, inv_sem)
    tell.start()
    load.wait()

    @pl.loop(0, count // step)
    def _(c):
        at = pl.ds(pl.multiple_of(c * step, step), step)
        to = pl.multiple_of(2 * c * step, 2 * step)
        table[pl.ds(to, step, stride=2), :] = rows[at, :lanes].astype(jnp.float32)
        table[pl.ds(to + 1, step, stride=2), :] = rows[at, lanes:].astype(jnp.float32)

    tell.wait()

    @pl.loop(0, blocks)
    def _(b):
        at = pl.multiple_of(2 * b * part, 2 * part)
        for r in range(part):
            i = pl.multiple_of(inv[b, r], 2)
            got[pl.ds(at + 2 * r, 2), :] = table[pl.ds(i, 2), :]

    width = 2 * lanes
    some = 4

    @pl.loop(0, out_ref.shape[0] // some)
    def _(g):
        at = pl.multiple_of(2 * g * some * own, 2 * some * own)
        a = got[pl.ds(at, some * own, stride=2), :]
        b = got[pl.ds(at + 1, some * own, stride=2), :]
        scale = lax.rsqrt(jnp.sum(a * a + b * b, axis=-1, keepdims=True) / width + norm_epsilon)
        to = pl.ds(g * some, some)
        out_ref[to, :own, :lanes] = (a * scale).astype(jnp.bfloat16).reshape(some, own, lanes)
        out_ref[to, :own, lanes:] = (b * scale).astype(jnp.bfloat16).reshape(some, own, lanes)


def slots_kernel(asked_ref, tile_ref, out_ref, sem):
    dests, slots = asked_ref.shape
    part = tile_ref.shape[1]
    for d in range(dests):
        for s in range(slots):
            pltpu.make_async_copy(tile_ref.at[asked_ref[d, s]], out_ref.at[d, pl.ds(s * part, part)], sem).start()
    pltpu.make_async_copy(out_ref, out_ref, sem).wait()


def one_slot_kernel(slot, asked_ref, tile_ref, out_ref, sem):
    for d in range(asked_ref.shape[0]):
        pltpu.make_async_copy(tile_ref.at[asked_ref[d, slot]], out_ref.at[d], sem).start()
    pltpu.make_async_copy(out_ref, out_ref, sem).wait()


def pick_kernel(slot_ref, arrived_ref, *refs):
    blocks, tiles = slot_ref.shape
    turns_ref, sem = refs[-2:]
    part = refs[0].shape[1]
    for n, out_ref in enumerate(refs[:-2]):
        for j in range(tiles):
            slot = slot_ref[n, j]
            row = pl.multiple_of(slot % 2 * part, part)
            pltpu.make_async_copy(
                arrived_ref.at[slot // 2, pl.ds(row, part)], out_ref.at[j], sem.at[n]
            ).start()
    one, two = (sum(slot_ref[n, j] % 2 for j in range(tiles)) for n in range(blocks))
    lead = jnp.where((one == 0) & (two > 0), 1, 0)
    turns_ref[0] = lead
    turns_ref[1] = jnp.where((one > 0) & (two > 0), 1, lead)
    for n, out_ref in enumerate(refs[:-2]):
        pltpu.make_async_copy(out_ref, out_ref, sem.at[n]).wait()


def first_pass_kernel(scale, y_ref, slot_ref, *refs):
    out_ref, total_ref, answer_ref, keys, values, key_sem, sems = refs[-7:]
    latents, first_ref, pieces = refs[:8], refs[8], refs[9:16]
    y = y_ref[0]
    blocks, tiles = slot_ref.shape
    rows = keys.shape[2]
    tile_part = rows // PLANES
    piece, block = pl.program_id(0), pl.program_id(1)

    @pl.when((piece == 0) & (block == 0))
    def _():
        for n in range(blocks):
            for turn, ref in enumerate(latents[n * PLANES : (n + 1) * PLANES]):
                row = pl.multiple_of((y + PLANES - turn) % PLANES * tile_part, tile_part)
                pltpu.make_async_copy(ref, keys.at[n, :, pl.ds(row, tile_part)], key_sem.at[n]).start()

            @pl.loop(0, tiles)
            def _(j):
                to = values.at[n, pl.ds(pl.multiple_of(j * rows, rows), rows)]
                pltpu.make_async_copy(first_ref.at[slot_ref[n, j] // 2], to, sems.at[n]).start()

    @pl.when(piece == 0)
    def _():
        pltpu.make_async_copy(keys.at[block], keys.at[block], key_sem.at[block]).wait()
        pltpu.make_async_copy(values.at[block], values.at[block], sems.at[block]).wait()

        @pl.loop(0, tiles)
        def _(j):
            @pl.when(slot_ref[block, j] % 2 == 1)
            def _():
                values[block, pl.ds(pl.multiple_of(j * rows, rows), rows), :] = jnp.zeros(
                    (rows, values.shape[2]), values.dtype
                )

    nt = (((1,), (1,)), ((), ()))
    group = 2
    span = group * rows
    q = pieces[0][...]
    for p in range(1, PLANES):
        other = jnp.concatenate([pieces[2 * p - 1][...], pieces[2 * p][...]], axis=0)
        q = jnp.where(piece == p, other, q)
    sources, part, width = q.shape
    q = q.reshape(sources * part, width)
    total = jnp.zeros((sources * part, rows), jnp.float32)
    weighted = jnp.zeros((sources * part, values.shape[2]), jnp.float32)
    for at in range(tiles // group):
        k = keys[block, at * group : (at + 1) * group].reshape(span, width)
        s = lax.dot_general(q, k, nt, preferred_element_type=jnp.float32)
        e = jnp.exp2(s * scale)
        for g in range(group):
            counted = (slot_ref[block, at * group + g] % 2 == 0).astype(jnp.float32)
            total = total + e[:, g * rows : (g + 1) * rows] * counted
        weighted = weighted + jnp.dot(
            e.astype(jnp.bfloat16), values[block, at * span : (at + 1) * span], preferred_element_type=jnp.float32
        )
    total = jnp.sum(total, axis=1, keepdims=True)
    out_ref[0] = weighted
    total_ref[0] = jnp.broadcast_to(total, total_ref.shape[1:])
    answer_ref[...] = (weighted * (1.0 / total)).astype(jnp.bfloat16).reshape(answer_ref.shape)


def finish_kernel(scale, turns_ref, y_ref, slot_ref, sum_ref, total_ref, *refs):
    pieces, latents, second_ref = refs[:7], refs[7:15], refs[15]
    out_ref, weighted, total, queries, keys, values, sems, tile_sem = refs[17:]
    y = y_ref[0]
    blocks, tiles = slot_ref.shape
    rows = keys.shape[1]
    tile_part = rows // PLANES
    turn_no, piece = pl.program_id(0), pl.program_id(1)
    block = turns_ref[turn_no]
    live = (turn_no == 0) | (block != turns_ref[0])
    sources, part, width = queries.shape[1:]
    chunk = 256

    @pl.when((piece == 0) & live)
    def _():
        for n in range(blocks):

            @pl.when(block == n)
            def _():
                @pl.loop(0, tiles)
                def _(j):
                    slot = slot_ref[n, j]

                    @pl.when(slot % 2 == 1)
                    def _():
                        for turn, ref in enumerate(latents[n * PLANES : (n + 1) * PLANES]):
                            row = pl.multiple_of((y + PLANES - turn) % PLANES * tile_part, tile_part)
                            pltpu.make_async_copy(ref.at[j], keys.at[j, pl.ds(row, tile_part)], tile_sem).start()
                        pltpu.make_async_copy(second_ref.at[slot // 2], values.at[j], tile_sem).start()

        own = pl.ds(pl.multiple_of(block * part, part), part)
        for p in range(PLANES):
            if p == 0:
                pltpu.make_async_copy(pieces[p].at[:, own], queries.at[p], sems.at[p]).start()
            else:
                mid = sources // 2
                for h in range(2):
                    to = queries.at[p, pl.ds(h * mid, mid)]
                    pltpu.make_async_copy(pieces[2 * p - 1 + h].at[:, own], to, sems.at[p]).start()
            for at in range(0, weighted.shape[1], chunk):
                some = pl.ds(at, chunk)
                pltpu.make_async_copy(sum_ref.at[blocks * p + block, some], weighted.at[p, some], sems.at[p]).start()
                pltpu.make_async_copy(total_ref.at[blocks * p + block, some], total.at[p, some], sems.at[p]).start()

        @pl.loop(0, tiles)
        def _(j):
            @pl.when(slot_ref[block, j] % 2 == 1)
            def _():
                pltpu.make_async_copy(keys.at[j], keys.at[j], tile_sem).wait()
                pltpu.make_async_copy(values.at[j], values.at[j], tile_sem).wait()

    @pl.when(live)
    def _():
        for held in (queries, weighted, total):
            pltpu.make_async_copy(held.at[piece], held.at[piece], sems.at[piece]).wait()
        nt = (((1,), (1,)), ((), ()))
        lanes = total.shape[2]

        @pl.loop(0, tiles)
        def _(j):
            @pl.when(slot_ref[block, j] % 2 == 1)
            def _():
                q = queries[piece].reshape(sources * part, width)
                s = lax.dot_general(q, keys[j], nt, preferred_element_type=jnp.float32)
                e = jnp.exp2(s * scale)
                total[piece] += jnp.sum(e, axis=1, keepdims=True)
                weighted[piece] += jnp.dot(e.astype(jnp.bfloat16), values[j], preferred_element_type=jnp.float32)

        share = 1.0 / total[piece]
        for at in range(0, weighted.shape[2], lanes):
            out_ref[:, :, at : at + lanes] = (
                (weighted[piece, :, at : at + lanes] * share).astype(jnp.bfloat16).reshape(sources, part, lanes)
            )


def unpack_kernel(pos_ref, in_ref, out_ref, table, got):
    lanes = 128
    step = 256
    count = out_ref.shape[0]
    begin = pl.program_id(0) * count

    @pl.when(pl.program_id(0) == 0)
    def _():
        @pl.loop(0, in_ref.shape[0] // step)
        def _(c):
            at = pl.ds(pl.multiple_of(c * step, step), step)
            to = pl.multiple_of(2 * c * step, 2 * step)
            table[pl.ds(to, step, stride=2), :] = in_ref[at, :lanes].astype(jnp.float32)
            table[pl.ds(to + 1, step, stride=2), :] = in_ref[at, lanes:].astype(jnp.float32)

    @pl.loop(0, count // 32)
    def _(c):
        at = pl.multiple_of(c * 64, 64)
        first = begin + c * 32
        for r in range(32):
            i = pl.multiple_of(pos_ref[0, first + r], 2)
            got[pl.ds(at + 2 * r, 2), :] = table[pl.ds(i, 2), :]

    @pl.loop(0, count // step)
    def _(c):
        at = pl.multiple_of(c * step, step)
        out_ref[pl.ds(at, step), :lanes] = got[pl.ds(2 * at, step, stride=2), :].astype(jnp.bfloat16)
        out_ref[pl.ds(at, step), lanes:] = got[pl.ds(2 * at + 1, step, stride=2), :].astype(jnp.bfloat16)


def shards(queries, cluster, anchor_latent, anchor_labels, tile_list):
    dp_count = lax.axis_size("dp")
    y = lax.axis_index("label").astype(jnp.int32)
    y1 = y.reshape(1)
    query_count, width = queries.shape
    blocks_here, tiles_each = tile_list.shape
    blocks = blocks_here * dp_count
    capacity = 2 * query_count // blocks
    part = capacity // PLANES
    tiles_here = anchor_latent.shape[0] // TILE
    tile_part = TILE // PLANES
    columns = anchor_labels.shape[1]
    wanted_count = blocks_here * tiles_each
    slots = 2

    wanted = tile_list.reshape(wanted_count)
    source = wanted // tiles_here
    number = jnp.arange(wanted_count, dtype=jnp.int32)
    order = jnp.sum(
        ((source[:, None] == source[None, :]) & (number[None, :] < number[:, None])).astype(jnp.int32), axis=1
    )
    slot_of = source * slots + order
    slot_table = slot_of.reshape(blocks_here, tiles_each)

    own = blocks_here * part
    sent, pos = pl.pallas_call(
        functools.partial(pack_kernel, blocks, part, tiles_here),
        in_specs=[SMEM, VMEM, VMEM, ANY],
        out_specs=[VMEM, VMEM],
        out_shape=[
            jax.ShapeDtypeStruct((dp_count, own + 8, width), jnp.bfloat16),
            jax.ShapeDtypeStruct((1, query_count), jnp.int32),
        ],
        scratch_shapes=[
            pltpu.VMEM((query_count, width), jnp.bfloat16),
            pltpu.VMEM((2 * query_count, 128), jnp.float32),
            pltpu.VMEM((2 * blocks * part, 128), jnp.float32),
            pltpu.VMEM((blocks, 128), jnp.int32),
            pltpu.SMEM((blocks, 128), jnp.int32),
            pltpu.SemaphoreType.DMA,
            pltpu.SemaphoreType.DMA,
        ],
        compiler_params=params(FULL),
        name="pack",
    )(y1, cluster.reshape(1, query_count), tile_list, queries)
    arrived = lax.all_to_all(sent, "dp", split_axis=0, concat_axis=0, tiled=True)
    asked = arrived[:, own, :: width // slots].astype(jnp.int32)

    quarter = lax.dynamic_slice_in_dim(anchor_latent.reshape(tiles_here, TILE, width), y * tile_part, tile_part, axis=1)
    label_tiles = anchor_labels.reshape(tiles_here, TILE, columns)

    def exchange(v):
        return lax.all_to_all(v, "dp", split_axis=0, concat_axis=0, tiled=True)

    def tiles_out(kernel, tiles, rows):
        return pl.pallas_call(
            kernel,
            in_specs=[SMEM, VMEM],
            out_specs=ANY,
            out_shape=jax.ShapeDtypeStruct((dp_count, rows, tiles.shape[2]), jnp.bfloat16),
            scratch_shapes=[pltpu.SemaphoreType.DMA],
            compiler_params=params(8),
        )(asked, tiles)

    got_latents = exchange(tiles_out(slots_kernel, unit_rows(quarter), slots * tile_part))
    first_out = tiles_out(functools.partial(one_slot_kernel, 0), label_tiles, TILE)
    second_out = tiles_out(functools.partial(one_slot_kernel, 1), label_tiles, TILE)

    def shift(v, by):
        return lax.ppermute(v, "label", [(i, (i + by) % PLANES) for i in range(PLANES)])

    mid = dp_count // 2
    q0a, q0b = arrived[:mid, :own], arrived[mid:, :own]
    q1a, q3b, q1b, q3a = shift(q0a, 1), shift(q0b, 3), shift(q0b, 1), shift(q0a, 3)
    got_first = exchange(first_out)
    *k0, turns = pl.pallas_call(
        pick_kernel,
        in_specs=[SMEM, ANY],
        out_specs=[VMEM] * blocks_here + [SMEM],
        out_shape=[jax.ShapeDtypeStruct((tiles_each, tile_part, width), jnp.bfloat16)] * blocks_here
        + [jax.ShapeDtypeStruct((blocks_here,), jnp.int32)],
        scratch_shapes=[pltpu.SemaphoreType.DMA((blocks_here,))],
        compiler_params=params(FULL),
        name="pick",
    )(slot_table, got_latents)
    k1a, k3b = shift(k0[0], 1), shift(k0[1], 3)
    k1b, k3a = shift(k0[1], 1), shift(k0[0], 3)
    k2a, k2b = shift(k1a, 1), shift(k3b, 3)
    got_second = exchange(second_out)
    latents = [k0[0], k1a, k2a, k3a, k0[1], k1b, k2b, k3b]
    q2a, q2b = shift(q1a, 1), shift(q3b, 3)

    rows = dp_count * part
    keys = tiles_each * TILE
    scale = LOG2E / (width * kernel_width)

    def rows_of(piece, sources):
        return pl.BlockSpec(
            (sources, part, width),
            lambda p, n: (0, jnp.where(p == piece, n, jnp.where(p < piece, 0, blocks_here - 1)), 0),
        )

    pieces = [arrived, q1a, q1b, q3a, q3b, q2a, q2b]
    *sums, answers = pl.pallas_call(
        functools.partial(first_pass_kernel, scale),
        grid=(PLANES, blocks_here),
        in_specs=[SMEM, SMEM]
        + [ANY] * 9
        + [rows_of(0, dp_count)]
        + [rows_of(p, mid) for p in range(1, PLANES) for _ in range(2)],
        out_specs=[
            pl.BlockSpec((1, rows, columns), lambda p, n: (blocks_here * p + n, 0, 0)),
            pl.BlockSpec((1, rows, 128), lambda p, n: (blocks_here * p + n, 0, 0)),
            pl.BlockSpec((dp_count, part, columns), lambda p, n: (0, blocks_here * p + n, 0)),
        ],
        out_shape=[
            jax.ShapeDtypeStruct((PLANES * blocks_here, rows, columns), jnp.float32),
            jax.ShapeDtypeStruct((PLANES * blocks_here, rows, 128), jnp.float32),
            jax.ShapeDtypeStruct((dp_count, PLANES * own, columns), jnp.bfloat16),
        ],
        scratch_shapes=[
            pltpu.VMEM((blocks_here, tiles_each, TILE, width), jnp.bfloat16),
            pltpu.VMEM((blocks_here, keys, columns), jnp.bfloat16),
            pltpu.SemaphoreType.DMA((blocks_here,)),
            pltpu.SemaphoreType.DMA((blocks_here,)),
        ],
        compiler_params=params(FULL),
        cost_estimate=pl.CostEstimate(
            flops=2 * PLANES * blocks_here * rows * keys * (width + columns),
            transcendentals=PLANES * blocks_here * rows * keys,
            bytes_accessed=6 * PLANES * blocks_here * rows * columns,
        ),
        name="first_pass",
    )(y1, slot_table, *latents, got_first, *pieces)

    def answer_block(n, p, t):
        repeated = (n > 0) & (t[n] == t[0])
        return (0, jnp.where(repeated, blocks_here * (PLANES - 1) + t[0], blocks_here * p + t[n]), 0)

    answers = pl.pallas_call(
        functools.partial(finish_kernel, scale),
        grid_spec=pltpu.PrefetchScalarGridSpec(
            num_scalar_prefetch=1,
            grid=(blocks_here, PLANES),
            in_specs=[SMEM, SMEM] + [ANY] * 19,
            out_specs=pl.BlockSpec((dp_count, part, columns), answer_block),
            scratch_shapes=[
                pltpu.VMEM((PLANES, rows, columns), jnp.float32),
                pltpu.VMEM((PLANES, rows, 128), jnp.float32),
                pltpu.VMEM((PLANES, dp_count, part, width), jnp.bfloat16),
                pltpu.VMEM((tiles_each, TILE, width), jnp.bfloat16),
                pltpu.VMEM((tiles_each, TILE, columns), jnp.bfloat16),
                pltpu.SemaphoreType.DMA((PLANES,)),
                pltpu.SemaphoreType.DMA,
            ],
        ),
        out_shape=jax.ShapeDtypeStruct((dp_count, PLANES * own, columns), jnp.bfloat16),
        input_output_aliases={5 + 7 + 9: 0},
        compiler_params=params(FULL),
        name="finish",
    )(turns, y1, slot_table, *sums, *pieces, *latents, got_second, answers)
    back = exchange(answers)
    count = back.shape[0] * back.shape[1]
    chunk = 1024
    return pl.pallas_call(
        unpack_kernel,
        grid=(query_count // chunk,),
        in_specs=[SMEM, VMEM],
        out_specs=pl.BlockSpec((chunk, columns), lambda c: (c, 0)),
        out_shape=jax.ShapeDtypeStruct((query_count, columns), jnp.bfloat16),
        scratch_shapes=[
            pltpu.VMEM((2 * count, 128), jnp.float32),
            pltpu.VMEM((2 * chunk, 128), jnp.float32),
        ],
        compiler_params=params(24),
        name="unpack",
    )(pos, back.reshape(count, columns))


def solution(mesh):
    placed = (P("dp", None), P("dp", None), P("dp", None), P("dp", "label"), P("dp", None))
    return jax.shard_map(shards, mesh=mesh, in_specs=placed, out_specs=P("dp", "label"), check_vma=False)
```
